32 devices in a mesh: row: 8 (over z, core), col: 4 (over y, x).
Axes of the slice: x: 2, y: 2, z: 4, core: 2. Of those that a mesh axis runs over, the one named last changes fastest.
Arguments:
- diag_tile: float32 [128, 128], P('row'), may hold values from -20 to 100, as said below
- panel: bfloat16 [16384, 128], P(('row', 'col')), may hold values from -1.796875 to 1.796875
- trailing: float32 [16384, 2048], P('row', 'col'), may hold values from -6 to 6
Outputs:
- solved: bfloat16 [16384, 128], P(('row', 'col'))
- updated: float32 [16384, 2048], P('row', 'col')
The draws below stay inside these ranges and needn't reach their ends.
Inputs may be any that keep to these rules, and one draw needn't show every extreme that they name: diag_tile is symmetric and positive definite, with its smallest eigenvalue 1 or more.
All inputs are finite; a program needn't handle non-finite values.
Results may differ from the reference program's by a relative error of at most 0.0051.
Values may be sent and summed in bfloat16 or wider, within the bound.
No kernel may reach another device: no remote copies, remote signals or barrier semaphores. Data moves between devices by JAX's collectives and lax.ppermute only.
A program may use at most 64 MiB of HBM per device.

```python
import math
import jax
import jax.numpy as jnp
from jax import lax

PANEL = 128
ROW_DEV = 2048
ROWS = 16384
COLS = 2048
N_ROW = 8


def draw_diag_tile(key, part):
    key_gram = jax.random.fold_in(key, 11)
    key_shift = jax.random.fold_in(key, 12)
    factor_draw = jax.random.normal(key_gram, (PANEL, PANEL), jnp.float32) / math.sqrt(PANEL)
    gram = jnp.dot(factor_draw, factor_draw.T, precision=lax.Precision.HIGHEST)
    gram = 0.5 * (gram + gram.T)
    shifts = jnp.exp(jax.random.uniform(key_shift, (PANEL,), jnp.float32, 0.0, math.log(4.0)))
    matrix_tile = gram + jnp.diag(shifts)
    return matrix_tile


def block_levels(key, dims, split, smallest, top_value):
    loudness = 1.0
    for dim, shards_of in split:
        heights = jax.random.uniform(jax.random.fold_in(jax.random.fold_in(key, 6), dim), (shards_of,), jnp.float32, smallest / len(split), top_value / len(split))
        loudness = loudness * jnp.repeat(jnp.exp(heights), dims[dim] // shards_of).reshape((-1,) + (1,) * (len(dims) - 1 - dim))
    return loudness


def gaussian(stream_key, dims, scale, bound, pieces=(), kind=jnp.bfloat16):
    drawn = jax.random.normal(stream_key, dims, jnp.float32) * scale
    if len(pieces) > 0:
        drawn = block_levels(stream_key, dims, pieces, -0.22, 0.18) * drawn
    return jnp.clip(drawn, min=-bound, max=bound).astype(kind)


def setup_inputs(seed: int = 0) -> dict:
    key_of = jax.random.split(jax.random.key(seed), 4)
    diag_tile = draw_diag_tile(jax.random.fold_in(key_of[3], 71), 0)
    panel = gaussian(key_of[1], (ROWS, PANEL), 0.3, 1.796875, ((0, 32),))
    trailing = gaussian(key_of[2], (ROWS, COLS), 1.0, 6.0, ((0, 8), (1, 4)), jnp.float32)
    return {"diag_tile": diag_tile, "panel": panel, "trailing": trailing}


def reference(diag_tile, panel, trailing):
    factor = jnp.linalg.cholesky(diag_tile)
    identity = jnp.eye(PANEL, dtype=diag_tile.dtype)
    inverse = lax.linalg.triangular_solve(factor, identity, left_side=True, lower=True).astype(jnp.bfloat16)
    solved = lax.dot_general(panel.astype(jnp.float32), inverse.astype(jnp.float32), (((1,), (1,)), ((), ())), preferred_element_type=jnp.float32).astype(jnp.bfloat16)
    top_rows = solved[:COLS]
    col_ids = jnp.arange(COLS, dtype=jnp.int32)

    def one_block(block_index):
        row_start = block_index * ROW_DEV
        block_rows = lax.dynamic_slice_in_dim(solved, row_start, ROW_DEV, 0)
        old_rows = lax.dynamic_slice_in_dim(trailing, row_start, ROW_DEV, 0)
        update = lax.dot_general(block_rows.astype(jnp.float32), top_rows.astype(jnp.float32), (((1,), (1,)), ((), ())), preferred_element_type=jnp.float32)
        row_ids = row_start + jnp.arange(ROW_DEV, dtype=jnp.int32)
        return jnp.where(row_ids[:, None] >= col_ids[None, :], old_rows - update, old_rows)
    blocks = lax.map(one_block, jnp.arange(N_ROW, dtype=jnp.int32))
    return (solved, blocks.reshape(ROWS, COLS))
```

```python
import functools

import jax
import jax.numpy as jnp
from jax import lax
from jax.experimental import pallas as pl
from jax.experimental.pallas import tpu as pltpu
from jax.sharding import PartitionSpec as P


SUB = 8
CHUNK = 256

VMEM = pl.BlockSpec(memory_space=pltpu.VMEM)
HBM = pl.BlockSpec(memory_space=pltpu.HBM)


def exchange(value, axis, size, step):
    return lax.ppermute(value, axis, [(i, i ^ step) for i in range(size)])


def far_steps(n_row):
    return [2 * i for i in reversed(range(1, n_row // 2))]


def inverse_factor(tile):
    n = tile[0].shape[1]
    blocks = n // SUB
    rows = list(tile)
    lane = lax.broadcasted_iota(jnp.int32, (SUB, n), 1)
    sub = lax.broadcasted_iota(jnp.int32, (SUB, n), 0)

    def col(x, c):
        return jnp.broadcast_to(x[:, c : c + 1], (SUB, n))

    def row(x, r):
        return jnp.broadcast_to(x[r : r + 1, :], (SUB, n))

    out = []
    for block in range(blocks):
        base = block * SUB
        inside = (lane >= base) & (lane < base + SUB)
        here = rows[block]
        cols = [col(here, base + j) for j in range(SUB)]
        here = jnp.where(inside, (lane - base == sub).astype(jnp.float32), here)
        more = block + 1 < blocks
        if more:
            after = rows[block + 1]
            cols_after = [col(after, base + j) for j in range(SUB)]
            after = jnp.where(inside, 0.0, after)
        pivots = jnp.zeros((SUB, n), jnp.float32)
        scales = jnp.zeros((SUB, n), jnp.float32)
        for k in range(0, SUB, 2):
            a, b, c = row(cols[k], k), row(cols[k + 1], k), row(cols[k + 1], k + 1)
            det = a * c - b * b
            inv_a = pl.reciprocal(a)
            inv_det = pl.reciprocal(det)
            ratio = b * inv_a
            first = row(here, k)
            second = row(here, k + 1) - ratio * first
            m1 = jnp.where(sub > k, cols[k], 0.0) * inv_a
            m2 = jnp.where(sub > k + 1, a * cols[k + 1] - b * cols[k], 0.0) * inv_det
            if more:
                n1 = cols_after[k] * inv_a
                n2 = (a * cols_after[k + 1] - b * cols_after[k]) * inv_det
            pairs = [(row(cols[j], k), row(cols[j], k + 1)) for j in range(k + 2, SUB)]
            for j, (x1, x2) in zip(range(k + 2, SUB), pairs):
                x2 = x2 - ratio * x1
                cols[j] = cols[j] - m1 * x1 - m2 * x2
                if more:
                    cols_after[j] = cols_after[j] - n1 * x1 - n2 * x2
            here = here - m1 * first - m2 * second
            if more:
                after = after - n1 * first - n2 * second
            pivots = jnp.where(sub == k, a, jnp.where(sub == k + 1, det * inv_a, pivots))
            scales = jnp.where(sub == k, inv_a, jnp.where(sub == k + 1, a * inv_det, scales))
        if more:
            rows[block + 1] = after
        if block + 2 < blocks:
            rest = lax.dot_general(
                here * scales,
                here,
                (((0,), (0,)), ((), ())),
                precision=lax.Precision.HIGHEST,
                preferred_element_type=jnp.float32,
            )
            for i in range(block + 2, blocks):
                rows[i] = jnp.where(inside, 0.0, rows[i]) - rest[i * SUB : (i + 1) * SUB]
        out.append(jnp.where(lane <= sub + base, here * lax.rsqrt(pivots), 0.0))
    return out


def inverse_kernel(n_row, *refs):
    trailing, own, *others = refs[: 1 + n_row // 2]
    out, held, tile, sem = refs[1 + n_row // 2 :]
    load = pltpu.make_async_copy(trailing, held, sem)
    load.start()
    me = lax.axis_index("row")
    depth = own.shape[0] // 2
    for step, piece in zip(range(0, n_row, 2), (own, *others)):
        for half in range(2):
            start = pl.multiple_of((me ^ step ^ half) * depth, depth)
            tile[pl.ds(start, depth), :] = piece[half * depth : (half + 1) * depth, :]
    n = tile.shape[0]
    blocks = inverse_factor([tile[i * SUB : (i + 1) * SUB, :] for i in range(n // SUB)])
    for i in range(0, n // SUB, 2):
        pair = jnp.concatenate([blocks[i], blocks[i + 1]], 0)
        out[i * SUB : (i + 2) * SUB, :] = pair.astype(out.dtype)
    load.wait()


def product(a, b):
    return lax.dot_general(a, b, (((1,), (1,)), ((), ())), preferred_element_type=jnp.float32)


def update_kernel(n_col, *refs):
    inverse, col_panel = refs[:2]
    pieces = refs[2 : 2 + n_col]
    trailing, solved, updated = refs[2 + n_col : 5 + n_col]
    new, col_solved, out_sems = refs[5 + n_col :]
    row, col = lax.axis_index("row"), lax.axis_index("col")
    rows_dev, cols_dev = trailing.shape
    depth = pieces[0].shape[0]
    chunk = min(CHUNK, depth)
    per_piece = depth // chunk

    def start_of(step, part):
        return pl.multiple_of((col ^ step) * depth + part * chunk, chunk)

    def store(step, part):
        span = pl.ds(start_of(step, part), chunk)
        return pltpu.make_async_copy(
            new.at[span], updated.at[span], out_sems.at[step * per_piece + part]
        )

    order = [(step, part) for step in range(n_col) for part in range(per_piece)]
    weights = inverse[...]
    col_solved[...] = product(col_panel[...], weights).astype(col_solved.dtype)
    for step, part in order:
        span = slice(part * chunk, (part + 1) * chunk)
        rows = product(pieces[step][span, :], weights).astype(solved.dtype)
        if step == 0:
            solved[span, :] = rows
        start = start_of(step, part)
        place = pl.ds(start, chunk)
        first_row = row * rows_dev + start
        first_col = col * cols_dev
        update = product(rows, col_solved[...])

        @pl.when(first_row >= first_col + cols_dev)
        def _():
            new[place, :] = trailing[place, :] - update

        @pl.when(first_row < first_col + cols_dev)
        def _():
            row_ids = first_row + lax.broadcasted_iota(jnp.int32, (chunk, cols_dev), 0)
            col_ids = first_col + lax.broadcasted_iota(jnp.int32, (chunk, cols_dev), 1)
            new[place, :] = trailing[place, :] - jnp.where(row_ids >= col_ids, update, 0.0)

        store(step, part).start()
    for step, part in order:
        store(step, part).wait()


def column_rows(panel, n_row, n_col, cols_dev):
    depth = panel.shape[0]
    rows_dev = depth * n_col
    row, col = lax.axis_index("row"), lax.axis_index("col")
    if depth == cols_dev and n_col * cols_dev <= rows_dev:
        half = depth // 2
        odd = row % 2 == 1
        beside = exchange(panel, "row", n_row, 1)
        mine = jnp.where(odd, beside[half:], panel[:half])
        part = mine
        for step in far_steps(n_row):
            came = exchange(mine, "row", n_row, step)
            part = jnp.where(row // 2 == step // 2, came, part)
        other = exchange(part, "row", n_row, 1)
        return jnp.where(
            odd, jnp.concatenate([other, part], 0), jnp.concatenate([part, other], 0)
        )
    whole = lax.all_gather(panel, "col", axis=0, tiled=True)
    start = col * cols_dev
    picked = lax.dynamic_slice_in_dim(whole, start % rows_dev, cols_dev, 0)
    kept = jnp.where(row == start // rows_dev, picked, 0).astype(picked.dtype)
    return lax.psum(kept, "row")


def per_device(n_row, n_col, diag_tile, panel, trailing):
    rows_dev, cols_dev = trailing.shape
    depth, width = panel.shape
    pieces = [panel] + [exchange(panel, "col", n_col, step) for step in range(1, n_col)]
    beside = exchange(diag_tile, "row", n_row, 1)
    two = jnp.concatenate([diag_tile, beside], 0)
    far = [exchange(two, "row", n_row, 2 * i) for i in range(1, n_row // 2)]
    inverse, held = pl.pallas_call(
        functools.partial(inverse_kernel, n_row),
        out_shape=(
            jax.ShapeDtypeStruct((width, width), jnp.bfloat16),
            jax.ShapeDtypeStruct(trailing.shape, trailing.dtype),
        ),
        in_specs=[HBM] + [VMEM] * (n_row // 2),
        out_specs=(VMEM, VMEM),
        scratch_shapes=[
            pltpu.VMEM((width, width), jnp.float32),
            pltpu.SemaphoreType.DMA,
        ],
        cost_estimate=pl.CostEstimate(
            flops=2 * width**3, bytes_accessed=width * width * 6, transcendentals=width
        ),
        compiler_params=pltpu.CompilerParams(vmem_limit_bytes=8 * 1024 * 1024),
        name="inverse",
    )(trailing, two, *far)
    col_panel = column_rows(panel, n_row, n_col, cols_dev)
    chunks = n_col * (depth // min(CHUNK, depth))
    return pl.pallas_call(
        functools.partial(update_kernel, n_col),
        out_shape=(
            jax.ShapeDtypeStruct(panel.shape, panel.dtype),
            jax.ShapeDtypeStruct(trailing.shape, trailing.dtype),
        ),
        in_specs=[VMEM] * (3 + n_col),
        out_specs=(VMEM, HBM),
        scratch_shapes=[
            pltpu.VMEM(trailing.shape, trailing.dtype),
            pltpu.VMEM((cols_dev, width), panel.dtype),
            pltpu.SemaphoreType.DMA((chunks,)),
        ],
        compiler_params=pltpu.CompilerParams(vmem_limit_bytes=24 * 1024 * 1024),
        cost_estimate=pl.CostEstimate(
            flops=2 * rows_dev * cols_dev * width,
            bytes_accessed=2 * rows_dev * cols_dev * 4,
            transcendentals=0,
        ),
        name="update",
    )(inverse, col_panel, *pieces, held)


def solution(mesh):
    n_row, n_col = mesh.shape["row"], mesh.shape["col"]
    in_specs = (P("row", None), P(("row", "col"), None), P("row", "col"))
    out_specs = (P(("row", "col"), None), P("row", "col"))

    def step(*args):
        return per_device(n_row, n_col, *args)

    return jax.shard_map(
        step, mesh=mesh, in_specs=in_specs, out_specs=out_specs, check_vma=False
    )
```

```python
import functools

import jax
import jax.numpy as jnp
from jax import lax
from jax.experimental import pallas as pl
from jax.experimental.pallas import tpu as pltpu
from jax.sharding import PartitionSpec as P


SUB = 8
CHUNK = 512

VMEM = pl.BlockSpec(memory_space=pltpu.VMEM)
HBM = pl.BlockSpec(memory_space=pltpu.HBM)


def exchange(value, axis, size, step):
    return lax.ppermute(value, axis, [(i, i ^ step) for i in range(size)])


def far_steps(n_row):
    return [2 * i for i in reversed(range(1, n_row // 2))]


def inverse_factor(tile):
    n = tile[0].shape[1]
    blocks = n // SUB
    rows = list(tile)
    lane = lax.broadcasted_iota(jnp.int32, (SUB, n), 1)
    sub = lax.broadcasted_iota(jnp.int32, (SUB, n), 0)

    def col(x, c):
        return jnp.broadcast_to(x[:, c : c + 1], (SUB, n))

    def row(x, r):
        return jnp.broadcast_to(x[r : r + 1, :], (SUB, n))

    out = []
    for block in range(blocks):
        base = block * SUB
        inside = (lane >= base) & (lane < base + SUB)
        here = rows[block]
        cols = [col(here, base + j) for j in range(SUB)]
        here = jnp.where(inside, (lane - base == sub).astype(jnp.float32), here)
        more = block + 1 < blocks
        if more:
            after = rows[block + 1]
            cols_after = [col(after, base + j) for j in range(SUB)]
            after = jnp.where(inside, 0.0, after)
        pivots = jnp.zeros((SUB, n), jnp.float32)
        scales = jnp.zeros((SUB, n), jnp.float32)
        for k in range(0, SUB, 2):
            a, b, c = row(cols[k], k), row(cols[k + 1], k), row(cols[k + 1], k + 1)
            det = a * c - b * b
            inv_a = pl.reciprocal(a)
            inv_det = pl.reciprocal(det)
            ratio = b * inv_a
            first = row(here, k)
            second = row(here, k + 1) - ratio * first
            m1 = jnp.where(sub > k, cols[k], 0.0) * inv_a
            m2 = jnp.where(sub > k + 1, a * cols[k + 1] - b * cols[k], 0.0) * inv_det
            if more:
                n1 = cols_after[k] * inv_a
                n2 = (a * cols_after[k + 1] - b * cols_after[k]) * inv_det
            pairs = [(row(cols[j], k), row(cols[j], k + 1)) for j in range(k + 2, SUB)]
            for j, (x1, x2) in zip(range(k + 2, SUB), pairs):
                x2 = x2 - ratio * x1
                cols[j] = cols[j] - m1 * x1 - m2 * x2
                if more:
                    cols_after[j] = cols_after[j] - n1 * x1 - n2 * x2
            here = here - m1 * first - m2 * second
            if more:
                after = after - n1 * first - n2 * second
            pivots = jnp.where(sub == k, a, jnp.where(sub == k + 1, det * inv_a, pivots))
            scales = jnp.where(sub == k, inv_a, jnp.where(sub == k + 1, a * inv_det, scales))
        if more:
            rows[block + 1] = after
        if block + 2 < blocks:
            rest = lax.dot_general(
                here * scales,
                here,
                (((0,), (0,)), ((), ())),
                precision=lax.Precision.HIGHEST,
                preferred_element_type=jnp.float32,
            )
            for i in range(block + 2, blocks):
                rows[i] = jnp.where(inside, 0.0, rows[i]) - rest[i * SUB : (i + 1) * SUB]
        out.append(jnp.where(lane <= sub + base, here * lax.rsqrt(pivots), 0.0))
    return out


def load_kernel(*refs):
    n = len(refs) // 2
    sems = refs[-1]
    copies = [
        pltpu.make_async_copy(refs[i], refs[n + i], sems.at[i]) for i in range(n)
    ]
    for copy in copies:
        copy.start()
    for copy in copies:
        copy.wait()


def pack_kernel(half, *refs):
    tile, tile_beside, *panels, out = refs
    me = lax.axis_index("row")
    odd = lax.rem(me, 2) == 1
    if half:
        panel, panel_beside = panels
        out[:half, :] = jnp.where(odd, panel_beside[half:, :], panel[:half, :])
    depth = tile.shape[0]
    for i, ref in enumerate((tile, tile_beside)):
        rest = ref[...]
        for term in range(3):
            start = half + (2 * term + i) * depth
            value = rest.astype(jnp.bfloat16)
            out[start : start + depth, :] = value
            rest = rest - value.astype(jnp.float32)


def inverse_kernel(n_row, half, *refs):
    trailing, *packs = refs[: 1 + n_row // 2]
    if half:
        near, out, held, tile, sem = refs[1 + n_row // 2 :]
    else:
        out, held, tile, sem = refs[1 + n_row // 2 :]
    load = pltpu.make_async_copy(trailing, held, sem)
    load.start()
    me = lax.axis_index("row")
    depth = tile.shape[0] // n_row
    for step, pack in zip(range(0, n_row, 2), packs):
        for i in range(2):
            terms = []
            for term in range(3):
                start = half + (2 * term + i) * depth
                terms.append(pack[start : start + depth, :].astype(jnp.float32))
            place = pl.multiple_of((me ^ step ^ i) * depth, depth)
            tile[pl.ds(place, depth), :] = (terms[0] + terms[1]) + terms[2]
        if half:

            @pl.when(me - lax.rem(me, 2) == step)
            def _():
                near[...] = pack[:half, :]

    @pl.when(me >= 0)
    def _():
        n = tile.shape[0]
        blocks = inverse_factor([tile[i * SUB : (i + 1) * SUB, :] for i in range(n // SUB)])
        for i in range(0, n // SUB, 2):
            pair = jnp.concatenate([blocks[i], blocks[i + 1]], 0)
            out[i * SUB : (i + 2) * SUB, :] = pair.astype(out.dtype)

    load.wait()


def product(a, b):
    return lax.dot_general(a, b, (((1,), (1,)), ((), ())), preferred_element_type=jnp.float32)


def update_kernel(n_col, first_half, *refs):
    if first_half:
        inverse, col_rows, held, *pieces = refs[: 3 + n_col]
        solved, solved_all, updated, new, col_solved, sems, own_sem = refs[3 + n_col :]
    else:
        inverse, col_rows, held, solved_all, _, updated, new, col_solved, sems, _ = refs
    row, col = lax.axis_index("row"), lax.axis_index("col")
    rows_dev, cols_dev = held.shape
    width = cols_dev // 2
    odd = lax.rem(row, 2)
    lanes = pl.multiple_of((odd if first_half else 1 - odd) * width, width)
    weights = inverse[...]
    col_solved[...] = product(col_rows[...], weights).astype(col_solved.dtype)
    if first_half:
        depth = pieces[0].shape[0]
        for step in range(n_col):
            place = pl.ds(pl.multiple_of((col ^ step) * depth, depth), depth)
            rows = product(pieces[step][...], weights)
            solved_all[place, :] = rows.astype(solved_all.dtype)
        own = pl.ds(pl.multiple_of(col * depth, depth), depth)
        save = pltpu.make_async_copy(solved_all.at[own], solved, own_sem)
        save.start()
    chunk = min(CHUNK, rows_dev)
    chunks = rows_dev // chunk
    ahead = row * rows_dev - (col * cols_dev + lanes)

    def store(i):
        place = pl.ds(pl.multiple_of(i * chunk, chunk), chunk)
        return pltpu.make_async_copy(
            new.at[place], updated.at[place, pl.ds(lanes, width)], sems.at[i]
        )

    @pl.loop(0, chunks)
    def _(i):
        start = pl.multiple_of(i * chunk, chunk)
        place = pl.ds(start, chunk)
        update = product(solved_all[place, :], col_solved[...])
        row_ids = lax.broadcasted_iota(jnp.int32, (chunk, width), 0)
        col_ids = lax.broadcasted_iota(jnp.int32, (chunk, width), 1)
        lower = col_ids - row_ids <= ahead + start
        old = held[place, pl.ds(lanes, width)]
        new[place, :] = old - jnp.where(lower, update, 0.0)
        store(i).start()

    @pl.loop(0, chunks)
    def _(i):
        store(i).wait()

    if first_half:
        save.wait()


def column_rows(panel, n_col, cols_dev):
    rows_dev = panel.shape[0] * n_col
    row, start = lax.axis_index("row"), lax.axis_index("col") * cols_dev
    whole = lax.all_gather(panel, "col", axis=0, tiled=True)
    picked = lax.dynamic_slice_in_dim(whole, start % rows_dev, cols_dev, 0)
    kept = jnp.where(row == start // rows_dev, picked, 0).astype(picked.dtype)
    rows = lax.psum(kept, "row")
    half = cols_dev // 2
    odd = row % 2 == 1
    return jnp.where(odd, rows[half:], rows[:half]), jnp.where(odd, rows[:half], rows[half:])


def per_device(n_row, n_col, diag_tile, panel, trailing):
    rows_dev, cols_dev = trailing.shape
    depth, width = panel.shape
    direct = depth == cols_dev and n_col * cols_dev <= rows_dev
    half = depth // 2 if direct else 0
    pieces = []
    for step in range(1, n_col):
        pieces.append(exchange(panel, "col", n_col, step))
    tile_near, panel_near = pl.pallas_call(
        load_kernel,
        out_shape=[jax.ShapeDtypeStruct(a.shape, a.dtype) for a in (diag_tile, panel)],
        in_specs=[HBM] * 2,
        out_specs=[VMEM] * 2,
        scratch_shapes=[pltpu.SemaphoreType.DMA((2,))],
        cost_estimate=pl.CostEstimate(flops=1, bytes_accessed=4 * depth * width, transcendentals=0),
        compiler_params=pltpu.CompilerParams(vmem_limit_bytes=4 * 1024 * 1024),
        name="load",
    )(diag_tile, panel)
    packed = [tile_near, exchange(diag_tile, "row", n_row, 1)]
    if direct:
        packed += [panel_near, exchange(panel, "row", n_row, 1)]
    pieces.insert(0, panel_near)
    pack_shape = (half + 6 * diag_tile.shape[0], width)
    pack = pl.pallas_call(
        functools.partial(pack_kernel, half),
        out_shape=jax.ShapeDtypeStruct(pack_shape, jnp.bfloat16),
        in_specs=[VMEM] * len(packed),
        out_specs=VMEM,
        cost_estimate=pl.CostEstimate(flops=1, bytes_accessed=4 * half * width, transcendentals=0),
        compiler_params=pltpu.CompilerParams(vmem_limit_bytes=4 * 1024 * 1024),
        name="pack",
    )(*packed)
    packs = {0: pack}
    for step in far_steps(n_row):
        packs[step] = exchange(pack, "row", n_row, step)
    packs = [packs[step] for step in range(0, n_row, 2)]
    outs = [
        jax.ShapeDtypeStruct((width, width), jnp.bfloat16),
        jax.ShapeDtypeStruct(trailing.shape, trailing.dtype),
    ]
    if direct:
        outs = [jax.ShapeDtypeStruct((half, width), panel.dtype)] + outs
    *near, inverse, held = pl.pallas_call(
        functools.partial(inverse_kernel, n_row, half),
        out_shape=outs,
        in_specs=[HBM] + [VMEM] * (n_row // 2),
        out_specs=[VMEM] * len(outs),
        scratch_shapes=[
            pltpu.VMEM((width, width), jnp.float32),
            pltpu.SemaphoreType.DMA,
        ],
        cost_estimate=pl.CostEstimate(
            flops=2 * width**3, bytes_accessed=width * width * 6, transcendentals=width
        ),
        compiler_params=pltpu.CompilerParams(vmem_limit_bytes=48 * 1024 * 1024),
        name="inverse",
    )(trailing, *packs)
    if direct:
        near = near[0]
        other = exchange(near, "row", n_row, 1)
    else:
        near, other = column_rows(panel, n_col, cols_dev)
    chunks = rows_dev // min(CHUNK, rows_dev)

    def update(first_half, operands, outs, out_specs, aliases):
        return pl.pallas_call(
            functools.partial(update_kernel, n_col, first_half),
            out_shape=outs,
            in_specs=[VMEM] * (len(operands) - len(aliases)) + [HBM] * len(aliases),
            out_specs=out_specs,
            scratch_shapes=[
                pltpu.VMEM((rows_dev, cols_dev // 2), trailing.dtype),
                pltpu.VMEM((cols_dev // 2, width), panel.dtype),
                pltpu.SemaphoreType.DMA((chunks,)),
                pltpu.SemaphoreType.DMA,
            ],
            input_output_aliases=aliases,
            compiler_params=pltpu.CompilerParams(vmem_limit_bytes=16 * 1024 * 1024),
            cost_estimate=pl.CostEstimate(
                flops=rows_dev * cols_dev * width,
                bytes_accessed=rows_dev * cols_dev * 4,
                transcendentals=0,
            ),
            name="update_first" if first_half else "update_second",
        )(*operands)

    slab = jax.ShapeDtypeStruct(trailing.shape, trailing.dtype)
    own = jax.ShapeDtypeStruct(panel.shape, panel.dtype)
    block = jax.ShapeDtypeStruct((rows_dev, width), panel.dtype)
    solved, solved_all, updated = update(
        True, (inverse, near, held, *pieces), (own, block, slab), (HBM, VMEM, HBM), {}
    )
    updated = update(
        False, (inverse, other, held, solved_all, updated), slab, HBM, {4: 0}
    )
    return solved, updated


def solution(mesh):
    n_row, n_col = mesh.shape["row"], mesh.shape["col"]
    in_specs = (P("row", None), P(("row", "col"), None), P("row", "col"))
    out_specs = (P(("row", "col"), None), P("row", "col"))

    def step(*args):
        return per_device(n_row, n_col, *args)

    return jax.shard_map(
        step, mesh=mesh, in_specs=in_specs, out_specs=out_specs, check_vma=False
    )
```

```python
import functools

import jax
import jax.numpy as jnp
from jax import lax
from jax.experimental import pallas as pl
from jax.experimental.pallas import tpu as pltpu
from jax.sharding import PartitionSpec as P


SUB = 8
AHEAD = 3
CHUNK = 1024

VMEM = pl.BlockSpec(memory_space=pltpu.VMEM)
HBM = pl.BlockSpec(memory_space=pltpu.HBM)


def exchange(value, axis, size, step):
    return lax.ppermute(value, axis, [(i, i ^ step) for i in range(size)])


def far_steps(n_row):
    half = n_row // 2
    return [half] + [i for i in range(n_row - 2, 0, -2) if i != half]


def terms(x):
    out = []
    for _ in range(3):
        out.append(x.astype(jnp.bfloat16).astype(jnp.float32))
        x = x - out[-1]
    return out


def outer_product(x, y):
    x, y = terms(x), terms(y)
    chosen = [(0, 0), (0, 1), (1, 0), (1, 1), (0, 2), (2, 0)]
    left = [x[i] for i, _ in chosen]
    right = [y[j] for _, j in chosen]
    left = jnp.concatenate(left, 0).astype(jnp.bfloat16)
    right = jnp.concatenate(right, 0).astype(jnp.bfloat16)
    return lax.dot_general(
        left, right, (((0,), (0,)), ((), ())), preferred_element_type=jnp.float32
    )


def inverse_factor(tile):
    n = tile[0].shape[1]
    blocks = n // SUB
    rows = list(tile)
    lane = lax.broadcasted_iota(jnp.int32, (SUB, n), 1)
    sub = lax.broadcasted_iota(jnp.int32, (SUB, n), 0)

    def col(x, c):
        return jnp.take_along_axis(x, jnp.full((SUB, n), c, jnp.int32), axis=1)

    def row(x, r):
        return jnp.broadcast_to(x[r : r + 1, :], (SUB, n))

    out = []
    for block in range(blocks):
        base = block * SUB
        inside = (lane >= base) & (lane < base + SUB)
        here = rows[block]
        cols = [col(here, base + j) for j in range(SUB)]
        here = jnp.where(inside, (lane - base == sub).astype(jnp.float32), here)
        near = range(block + 1, min(block + 1 + AHEAD, blocks))
        cols_near = {i: [col(rows[i], base + j) for j in range(SUB)] for i in near}
        for i in near:
            rows[i] = jnp.where(inside, 0.0, rows[i])
        pivots = jnp.zeros((SUB, n), jnp.float32)
        scales = jnp.zeros((SUB, n), jnp.float32)
        for k in range(0, SUB, 2):
            a, b, c = row(cols[k], k), row(cols[k + 1], k), row(cols[k + 1], k + 1)
            det = a * c - b * b
            inv_a = pl.reciprocal(a)
            inv_det = pl.reciprocal(det)
            ratio = b * inv_a
            first = row(here, k)
            second = row(here, k + 1) - ratio * first
            m1 = jnp.where(sub > k, cols[k], 0.0) * inv_a
            m2 = jnp.where(sub > k + 1, a * cols[k + 1] - b * cols[k], 0.0) * inv_det
            n1 = {i: cols_near[i][k] * inv_a for i in near}
            n2 = {i: (a * cols_near[i][k + 1] - b * cols_near[i][k]) * inv_det for i in near}
            pairs = [(row(cols[j], k), row(cols[j], k + 1)) for j in range(k + 2, SUB)]
            for j, (x1, x2) in zip(range(k + 2, SUB), pairs):
                x2 = x2 - ratio * x1
                cols[j] = cols[j] - m1 * x1 - m2 * x2
                for i in near:
                    cols_near[i][j] = cols_near[i][j] - n1[i] * x1 - n2[i] * x2
            here = here - m1 * first - m2 * second
            for i in near:
                rows[i] = rows[i] - n1[i] * first - n2[i] * second
            pivots = jnp.where(sub == k, a, jnp.where(sub == k + 1, det * inv_a, pivots))
            scales = jnp.where(sub == k, inv_a, jnp.where(sub == k + 1, a * inv_det, scales))
        far = range(block + 1 + AHEAD, blocks)
        if far:
            rest = outer_product(here * scales, here)
            for i in far:
                rows[i] = jnp.where(inside, 0.0, rows[i]) - rest[i * SUB : (i + 1) * SUB]
        out.append(jnp.where(lane <= sub + base, here * lax.rsqrt(pivots), 0.0))
    return out


def load_kernel(*refs):
    n = len(refs) // 2
    sems = refs[-1]
    copies = [
        pltpu.make_async_copy(refs[i], refs[n + i], sems.at[i]) for i in range(n)
    ]
    for copy in copies:
        copy.start()
    for copy in copies:
        copy.wait()


def pack_kernel(half, *refs):
    tile, tile_beside, *panels, out = refs
    me = lax.axis_index("row")
    odd = lax.rem(me, 2) == 1
    if half:
        panel, panel_beside = panels
        out[:half, :] = jnp.where(odd, panel_beside[half:, :], panel[:half, :])
    depth = tile.shape[0]
    for i, ref in enumerate((tile, tile_beside)):
        rest = ref[...]
        for term in range(3):
            start = half + (2 * term + i) * depth
            value = rest.astype(jnp.bfloat16)
            out[start : start + depth, :] = value
            rest = rest - value.astype(jnp.float32)


def inverse_kernel(n_row, half, *refs):
    trailing, *packs = refs[: 1 + n_row // 2]
    if half:
        near, out, held, tile, sem = refs[1 + n_row // 2 :]
    else:
        out, held, tile, sem = refs[1 + n_row // 2 :]
    load = pltpu.make_async_copy(trailing, held, sem)
    load.start()
    me = lax.axis_index("row")
    depth = tile.shape[0] // n_row
    for step, pack in zip(range(0, n_row, 2), packs):
        for i in range(2):
            terms = []
            for term in range(3):
                start = half + (2 * term + i) * depth
                terms.append(pack[start : start + depth, :].astype(jnp.float32))
            place = pl.multiple_of((me ^ step ^ i) * depth, depth)
            tile[pl.ds(place, depth), :] = (terms[0] + terms[1]) + terms[2]
        if half:

            @pl.when(me - lax.rem(me, 2) == step)
            def _():
                near[...] = pack[:half, :]

    @pl.when(me >= 0)
    def _():
        n = tile.shape[0]
        blocks = inverse_factor([tile[i * SUB : (i + 1) * SUB, :] for i in range(n // SUB)])
        for i in range(0, n // SUB, 2):
            pair = jnp.concatenate([blocks[i], blocks[i + 1]], 0)
            out[i * SUB : (i + 2) * SUB, :] = pair.astype(out.dtype)

    load.wait()


def product(a, b):
    return lax.dot_general(a, b, (((1,), (1,)), ((), ())), preferred_element_type=jnp.float32)


def update_kernel(n_col, first_half, *refs):
    if first_half:
        inverse, col_rows, held, *pieces = refs[: 3 + n_col]
        solved, solved_all, updated, new, col_solved, sems, own_sem = refs[3 + n_col :]
    else:
        inverse, col_rows, held, solved_all, _, updated, new, col_solved, sems, _ = refs
    row, col = lax.axis_index("row"), lax.axis_index("col")
    rows_dev, cols_dev = held.shape
    width = cols_dev // 2
    odd = lax.rem(row, 2)
    lanes = pl.multiple_of((odd if first_half else 1 - odd) * width, width)
    weights = inverse[...]
    col_solved[...] = product(col_rows[...], weights).astype(col_solved.dtype)
    if first_half:
        depth = pieces[0].shape[0]
        for step in range(n_col):
            place = pl.ds(pl.multiple_of((col ^ step) * depth, depth), depth)
            rows = product(pieces[step][...], weights)
            solved_all[place, :] = rows.astype(solved_all.dtype)
        own = pl.ds(pl.multiple_of(col * depth, depth), depth)
        save = pltpu.make_async_copy(solved_all.at[own], solved, own_sem)
        save.start()
    chunk = min(CHUNK, rows_dev)
    chunks = rows_dev // chunk
    ahead = row * rows_dev - (col * cols_dev + lanes)

    def store(i):
        place = pl.ds(pl.multiple_of(i * chunk, chunk), chunk)
        return pltpu.make_async_copy(
            new.at[place], updated.at[place, pl.ds(lanes, width)], sems.at[i]
        )

    @pl.loop(0, chunks)
    def _(i):
        start = pl.multiple_of(i * chunk, chunk)
        place = pl.ds(start, chunk)
        update = product(solved_all[place, :], col_solved[...])
        row_ids = lax.broadcasted_iota(jnp.int32, (chunk, width), 0)
        col_ids = lax.broadcasted_iota(jnp.int32, (chunk, width), 1)
        lower = col_ids - row_ids <= ahead + start
        old = held[place, pl.ds(lanes, width)]
        new[place, :] = old - jnp.where(lower, update, 0.0)
        store(i).start()

    @pl.loop(0, chunks)
    def _(i):
        store(i).wait()

    if first_half:
        save.wait()


def column_rows(panel, n_col, cols_dev):
    rows_dev = panel.shape[0] * n_col
    row, start = lax.axis_index("row"), lax.axis_index("col") * cols_dev
    whole = lax.all_gather(panel, "col", axis=0, tiled=True)
    picked = lax.dynamic_slice_in_dim(whole, start % rows_dev, cols_dev, 0)
    kept = jnp.where(row == start // rows_dev, picked, 0).astype(picked.dtype)
    rows = lax.psum(kept, "row")
    half = cols_dev // 2
    odd = row % 2 == 1
    return jnp.where(odd, rows[half:], rows[:half]), jnp.where(odd, rows[:half], rows[half:])


def per_device(n_row, n_col, diag_tile, panel, trailing):
    rows_dev, cols_dev = trailing.shape
    depth, width = panel.shape
    direct = depth == cols_dev and n_col * cols_dev <= rows_dev
    half = depth // 2 if direct else 0
    pieces = []
    for step in range(1, n_col):
        pieces.append(exchange(panel, "col", n_col, step))
    tile_near, panel_near = pl.pallas_call(
        load_kernel,
        out_shape=[jax.ShapeDtypeStruct(a.shape, a.dtype) for a in (diag_tile, panel)],
        in_specs=[HBM] * 2,
        out_specs=[VMEM] * 2,
        scratch_shapes=[pltpu.SemaphoreType.DMA((2,))],
        cost_estimate=pl.CostEstimate(flops=1, bytes_accessed=4 * depth * width, transcendentals=0),
        compiler_params=pltpu.CompilerParams(vmem_limit_bytes=4 * 1024 * 1024),
        name="load",
    )(diag_tile, panel)
    packed = [tile_near, exchange(diag_tile, "row", n_row, 1)]
    if direct:
        packed += [panel_near, exchange(panel, "row", n_row, 1)]
    pieces.insert(0, panel_near)
    pack_shape = (half + 6 * diag_tile.shape[0], width)
    pack = pl.pallas_call(
        functools.partial(pack_kernel, half),
        out_shape=jax.ShapeDtypeStruct(pack_shape, jnp.bfloat16),
        in_specs=[VMEM] * len(packed),
        out_specs=VMEM,
        cost_estimate=pl.CostEstimate(flops=1, bytes_accessed=4 * half * width, transcendentals=0),
        compiler_params=pltpu.CompilerParams(vmem_limit_bytes=4 * 1024 * 1024),
        name="pack",
    )(*packed)
    packs = {0: pack}
    for step in far_steps(n_row):
        packs[step] = exchange(pack, "row", n_row, step)
    packs = [packs[step] for step in range(0, n_row, 2)]
    outs = [
        jax.ShapeDtypeStruct((width, width), jnp.bfloat16),
        jax.ShapeDtypeStruct(trailing.shape, trailing.dtype),
    ]
    if direct:
        outs = [jax.ShapeDtypeStruct((half, width), panel.dtype)] + outs
    *near, inverse, held = pl.pallas_call(
        functools.partial(inverse_kernel, n_row, half),
        out_shape=outs,
        in_specs=[HBM] + [VMEM] * (n_row // 2),
        out_specs=[VMEM] * len(outs),
        scratch_shapes=[
            pltpu.VMEM((width, width), jnp.float32),
            pltpu.SemaphoreType.DMA,
        ],
        cost_estimate=pl.CostEstimate(
            flops=2 * width**3, bytes_accessed=width * width * 6, transcendentals=width
        ),
        compiler_params=pltpu.CompilerParams(vmem_limit_bytes=48 * 1024 * 1024),
        name="inverse",
    )(trailing, *packs)
    if direct:
        near = near[0]
        other = exchange(near, "row", n_row, 1)
    else:
        near, other = column_rows(panel, n_col, cols_dev)
    chunks = rows_dev // min(CHUNK, rows_dev)

    def update(first_half, operands, outs, out_specs, aliases):
        return pl.pallas_call(
            functools.partial(update_kernel, n_col, first_half),
            out_shape=outs,
            in_specs=[VMEM] * (len(operands) - len(aliases)) + [HBM] * len(aliases),
            out_specs=out_specs,
            scratch_shapes=[
                pltpu.VMEM((rows_dev, cols_dev // 2), trailing.dtype),
                pltpu.VMEM((cols_dev // 2, width), panel.dtype),
                pltpu.SemaphoreType.DMA((chunks,)),
                pltpu.SemaphoreType.DMA,
            ],
            input_output_aliases=aliases,
            compiler_params=pltpu.CompilerParams(vmem_limit_bytes=16 * 1024 * 1024),
            cost_estimate=pl.CostEstimate(
                flops=rows_dev * cols_dev * width,
                bytes_accessed=rows_dev * cols_dev * 4,
                transcendentals=0,
            ),
            name="update_first" if first_half else "update_second",
        )(*operands)

    slab = jax.ShapeDtypeStruct(trailing.shape, trailing.dtype)
    own = jax.ShapeDtypeStruct(panel.shape, panel.dtype)
    block = jax.ShapeDtypeStruct((rows_dev, width), panel.dtype)
    solved, solved_all, updated = update(
        True, (inverse, near, held, *pieces), (own, block, slab), (HBM, VMEM, HBM), {}
    )
    updated = update(
        False, (inverse, other, held, solved_all, updated), slab, HBM, {4: 0}
    )
    return solved, updated


def solution(mesh):
    n_row, n_col = mesh.shape["row"], mesh.shape["col"]
    in_specs = (P("row", None), P(("row", "col"), None), P("row", "col"))
    out_specs = (P(("row", "col"), None), P("row", "col"))

    def step(*args):
        return per_device(n_row, n_col, *args)

    return jax.shard_map(
        step, mesh=mesh, in_specs=in_specs, out_specs=out_specs, check_vma=False
    )
```

```python
import functools

import jax
import jax.numpy as jnp
from jax import lax
from jax.experimental import pallas as pl
from jax.experimental.pallas import tpu as pltpu
from jax.sharding import PartitionSpec as P


SUB = 8
AHEAD = 3

VMEM = pl.BlockSpec(memory_space=pltpu.VMEM)
HBM = pl.BlockSpec(memory_space=pltpu.HBM)


def exchange(value, axis, size, step):
    return lax.ppermute(value, axis, [(i, i ^ step) for i in range(size)])


def far_steps(n_row):
    half = n_row // 2
    return [half] + [i for i in range(n_row - 2, 0, -2) if i != half]


def terms(x):
    out = []
    for _ in range(3):
        out.append(x.astype(jnp.bfloat16).astype(jnp.float32))
        x = x - out[-1]
    return out


def outer_product(x, y):
    x, y = terms(x), terms(y)
    chosen = [(0, 0), (0, 1), (1, 0), (1, 1), (0, 2), (2, 0)]
    left = [x[i] for i, _ in chosen]
    right = [y[j] for _, j in chosen]
    left = jnp.concatenate(left, 0).astype(jnp.bfloat16)
    right = jnp.concatenate(right, 0).astype(jnp.bfloat16)
    return lax.dot_general(
        left, right, (((0,), (0,)), ((), ())), preferred_element_type=jnp.float32
    )


def tree_steps(n_row):
    steps = [n_row // 4]
    while steps[-1] > 2:
        steps.append(steps[-1] // 2)
    return steps


def inverse_factor(tile):
    n = tile[0].shape[1]
    blocks = n // SUB
    rows = list(tile)
    lane = lax.broadcasted_iota(jnp.int32, (SUB, n), 1)
    sub = lax.broadcasted_iota(jnp.int32, (SUB, n), 0)

    def col(x, c):
        return jnp.take_along_axis(x, jnp.full((SUB, n), c, jnp.int32), axis=1)

    def row(x, r):
        return jnp.broadcast_to(x[r : r + 1, :], (SUB, n))

    out = []
    for block in range(blocks):
        base = block * SUB
        inside = (lane >= base) & (lane < base + SUB)
        here = rows[block]
        cols = [col(here, base + j) for j in range(SUB)]
        here = jnp.where(inside, (lane - base == sub).astype(jnp.float32), here)
        near = range(block + 1, min(block + 1 + AHEAD, blocks))
        cols_near = {i: [col(rows[i], base + j) for j in range(SUB)] for i in near}
        for i in near:
            rows[i] = jnp.where(inside, 0.0, rows[i])
        pivots = jnp.zeros((SUB, n), jnp.float32)
        scales = jnp.zeros((SUB, n), jnp.float32)
        for k in range(0, SUB, 2):
            a, b, c = row(cols[k], k), row(cols[k + 1], k), row(cols[k + 1], k + 1)
            det = a * c - b * b
            inv_a = pl.reciprocal(a)
            inv_det = pl.reciprocal(det)
            ratio = b * inv_a
            first = row(here, k)
            second = row(here, k + 1) - ratio * first
            m1 = jnp.where(sub > k, cols[k], 0.0) * inv_a
            m2 = jnp.where(sub > k + 1, a * cols[k + 1] - b * cols[k], 0.0) * inv_det
            n1 = {i: cols_near[i][k] * inv_a for i in near}
            n2 = {i: (a * cols_near[i][k + 1] - b * cols_near[i][k]) * inv_det for i in near}
            pairs = [(row(cols[j], k), row(cols[j], k + 1)) for j in range(k + 2, SUB)]
            for j, (x1, x2) in zip(range(k + 2, SUB), pairs):
                x2 = x2 - ratio * x1
                cols[j] = cols[j] - m1 * x1 - m2 * x2
                for i in near:
                    cols_near[i][j] = cols_near[i][j] - n1[i] * x1 - n2[i] * x2
            here = here - m1 * first - m2 * second
            for i in near:
                rows[i] = rows[i] - n1[i] * first - n2[i] * second
            pivots = jnp.where(sub == k, a, jnp.where(sub == k + 1, det * inv_a, pivots))
            scales = jnp.where(sub == k, inv_a, jnp.where(sub == k + 1, a * inv_det, scales))
        far = range(block + 1 + AHEAD, blocks)
        if far:
            rest = outer_product(here * scales, here)
            for i in far:
                rows[i] = jnp.where(inside, 0.0, rows[i]) - rest[i * SUB : (i + 1) * SUB]
        out.append(jnp.where(lane <= sub + base, here * lax.rsqrt(pivots), 0.0))
    return out


def load_kernel(*refs):
    n = len(refs) // 2
    sems = refs[-1]
    copies = [
        pltpu.make_async_copy(refs[i], refs[n + i], sems.at[i]) for i in range(n)
    ]
    for copy in copies:
        copy.start()
    for copy in copies:
        copy.wait()


def pack_kernel(half, *refs):
    if half:
        tile, tile_beside, panel, panel_beside, two, pack = refs
        odd = lax.rem(lax.axis_index("row"), 2) == 1
        pack[:half, :] = jnp.where(odd, panel_beside[half:, :], panel[:half, :])
    else:
        tile, tile_beside, two = refs
    depth = tile.shape[0]
    for i, ref in enumerate((tile, tile_beside)):
        two[i * depth : (i + 1) * depth, :] = ref[...]
        if half:
            for term, value in enumerate(terms(ref[...])):
                start = half + (2 * term + i) * depth
                pack[start : start + depth, :] = value.astype(jnp.bfloat16)


def inverse_kernel(n_row, half, *refs):
    trailing, *packs, out, held, tile, sem = refs
    load = pltpu.make_async_copy(trailing, held, sem)
    load.start()
    me = lax.axis_index("row")
    depth = tile.shape[0] // n_row
    for step, pack in zip(range(0, n_row, 2), packs):
        for i in range(2):
            if pack.dtype == tile.dtype:
                value = pack[i * depth : (i + 1) * depth, :]
            else:
                parts = []
                for term in range(3):
                    start = half + (2 * term + i) * depth
                    parts.append(pack[start : start + depth, :].astype(jnp.float32))
                value = (parts[0] + parts[1]) + parts[2]
            place = pl.multiple_of((me ^ step ^ i) * depth, depth)
            tile[pl.ds(place, depth), :] = value

    @pl.when(me >= 0)
    def _():
        n = tile.shape[0]
        blocks = inverse_factor([tile[i * SUB : (i + 1) * SUB, :] for i in range(n // SUB)])
        for i in range(0, n // SUB, 2):
            pair = jnp.concatenate([blocks[i], blocks[i + 1]], 0)
            out[i * SUB : (i + 2) * SUB, :] = pair.astype(out.dtype)

    load.wait()


def product(a, b):
    return lax.dot_general(a, b, (((1,), (1,)), ((), ())), preferred_element_type=jnp.float32)


def update_kernel(n_col, first, *refs):
    early = n_col // 2
    count = early if first else n_col - early
    inverse, col_rows, held = refs[:3]
    pieces, refs = refs[3 : 3 + count], refs[3 + count :]
    if first:
        solved, all_rows, cols_near, updated, new, sems, own_sem = refs
    else:
        early_rows, cols_near, _, updated, new, sems, cols_other, all_rows = refs
    row, col = lax.axis_index("row"), lax.axis_index("col")
    rows_dev, cols_dev = held.shape
    width = cols_dev // 2
    depth = rows_dev // n_col
    odd = lax.rem(row, 2)
    lanes_near = pl.multiple_of(odd * width, width)
    lanes_other = pl.multiple_of((1 - odd) * width, width)
    weights = inverse[...]

    def place_of(step):
        return pl.ds(pl.multiple_of((col ^ step) * depth, depth), depth)

    def store(step, lanes, slot):
        return pltpu.make_async_copy(
            new.at[pl.ds(slot * depth, depth)],
            updated.at[place_of(step), pl.ds(lanes, width)],
            sems.at[slot],
        )

    def block(step, rows, cols, lanes, slot):
        place = place_of(step)
        update = product(rows[...], cols[...])
        ahead = row * rows_dev + (col ^ step) * depth - (col * cols_dev + lanes)
        row_ids = lax.broadcasted_iota(jnp.int32, (depth, width), 0)
        col_ids = lax.broadcasted_iota(jnp.int32, (depth, width), 1)
        old = held[place, pl.ds(lanes, width)]
        new[pl.ds(slot * depth, depth), :] = old - jnp.where(
            col_ids - row_ids <= ahead, update, 0.0
        )
        store(step, lanes, slot).start()

    cols = cols_near if first else cols_other
    cols[...] = product(col_rows[...], weights).astype(cols.dtype)

    def solve():
        for i in range(count):
            rows = product(pieces[i][...], weights)
            all_rows[i * depth : (i + 1) * depth, :] = rows.astype(all_rows.dtype)

    def part(i):
        return pl.ds(pl.multiple_of(i * depth, depth), depth)

    if first:
        solve()
        save = pltpu.make_async_copy(all_rows.at[part(0)], solved, own_sem)
        save.start()

        @pl.loop(0, early)
        def _(i):
            block(i, all_rows.at[part(i)], cols_near, lanes_near, i)

        @pl.loop(0, early)
        def _(i):
            store(i, lanes_near, i).wait()

        save.wait()
    else:

        @pl.loop(0, early)
        def _(i):
            block(i, early_rows.at[part(i)], cols_other, lanes_other, i)

        solve()

        @pl.loop(0, count)
        def _(i):
            block(early + i, all_rows.at[part(i)], cols_near, lanes_near, n_col + i)
            block(early + i, all_rows.at[part(i)], cols_other, lanes_other, early + i)

        @pl.loop(0, n_col)
        def _(i):
            store(i, lanes_other, i).wait()

        @pl.loop(0, count)
        def _(i):
            store(early + i, lanes_near, n_col + i).wait()


def column_rows(panel, n_col, cols_dev):
    rows_dev = panel.shape[0] * n_col
    row, start = lax.axis_index("row"), lax.axis_index("col") * cols_dev
    whole = lax.all_gather(panel, "col", axis=0, tiled=True)
    picked = lax.dynamic_slice_in_dim(whole, start % rows_dev, cols_dev, 0)
    kept = jnp.where(row == start // rows_dev, picked, 0).astype(picked.dtype)
    rows = lax.psum(kept, "row")
    half = cols_dev // 2
    odd = row % 2 == 1
    return jnp.where(odd, rows[half:], rows[:half]), jnp.where(odd, rows[:half], rows[half:])


def per_device(n_row, n_col, diag_tile, panel, trailing):
    rows_dev, cols_dev = trailing.shape
    depth, width = panel.shape
    direct = depth == cols_dev and n_col * cols_dev <= rows_dev
    half = depth // 2 if direct else 0
    pieces = []
    for step in range(1, n_col):
        pieces.append(exchange(panel, "col", n_col, step))
    tile_near, panel_near = pl.pallas_call(
        load_kernel,
        out_shape=[jax.ShapeDtypeStruct(a.shape, a.dtype) for a in (diag_tile, panel)],
        in_specs=[HBM] * 2,
        out_specs=[VMEM] * 2,
        scratch_shapes=[pltpu.SemaphoreType.DMA((2,))],
        cost_estimate=pl.CostEstimate(flops=1, bytes_accessed=4 * depth * width, transcendentals=0),
        compiler_params=pltpu.CompilerParams(vmem_limit_bytes=4 * 1024 * 1024),
        name="load",
    )(
        pltpu.with_memory_space_constraint(diag_tile, pltpu.HBM),
        pltpu.with_memory_space_constraint(panel, pltpu.HBM),
    )
    packed = [tile_near, exchange(diag_tile, "row", n_row, 1)]
    outs = [jax.ShapeDtypeStruct((2 * diag_tile.shape[0], width), jnp.float32)]
    if direct:
        packed += [panel_near, exchange(panel, "row", n_row, 1)]
        pack_shape = (half + 6 * diag_tile.shape[0], width)
        outs.append(jax.ShapeDtypeStruct(pack_shape, panel.dtype))
    pieces.insert(0, panel_near)
    two, *pack = pl.pallas_call(
        functools.partial(pack_kernel, half),
        out_shape=outs,
        in_specs=[VMEM] * len(packed),
        out_specs=[VMEM] * len(outs),
        cost_estimate=pl.CostEstimate(flops=1, bytes_accessed=4 * depth * width, transcendentals=0),
        compiler_params=pltpu.CompilerParams(vmem_limit_bytes=4 * 1024 * 1024),
        name="pack",
    )(*packed)
    middle = n_row // 2
    packs = {0: two}
    for step in far_steps(n_row):
        value = pack[0] if direct and step == middle else two
        packs[step] = exchange(value, "row", n_row, step)
    row = lax.axis_index("row")
    if direct:
        near = jnp.where(row & middle != 0, packs[middle][:half], pack[0][:half])
        for step in tree_steps(n_row):
            came = exchange(near, "row", n_row, step)
            near = jnp.where(row & step != 0, came, near)
        other = exchange(near, "row", n_row, 1)
    else:
        near, other = column_rows(panel, n_col, cols_dev)
    packs = [packs[step] for step in range(0, n_row, 2)]
    inverse, held = pl.pallas_call(
        functools.partial(inverse_kernel, n_row, half),
        out_shape=[
            jax.ShapeDtypeStruct((width, width), jnp.bfloat16),
            jax.ShapeDtypeStruct(trailing.shape, trailing.dtype),
        ],
        in_specs=[HBM] + [VMEM] * (n_row // 2),
        out_specs=[VMEM] * 2,
        scratch_shapes=[
            pltpu.VMEM((width, width), jnp.float32),
            pltpu.SemaphoreType.DMA,
        ],
        cost_estimate=pl.CostEstimate(
            flops=2 * width**3, bytes_accessed=width * width * 6, transcendentals=width
        ),
        compiler_params=pltpu.CompilerParams(vmem_limit_bytes=48 * 1024 * 1024),
        name="inverse",
    )(trailing, *packs)

    early = n_col // 2
    late = n_col - early
    slab = jax.ShapeDtypeStruct(trailing.shape, trailing.dtype)
    own = jax.ShapeDtypeStruct(panel.shape, panel.dtype)
    early_rows = jax.ShapeDtypeStruct((early * depth, width), panel.dtype)
    cols_near = jax.ShapeDtypeStruct((cols_dev // 2, width), panel.dtype)
    params = dict(
        compiler_params=pltpu.CompilerParams(vmem_limit_bytes=16 * 1024 * 1024),
        cost_estimate=pl.CostEstimate(
            flops=rows_dev * cols_dev * width,
            bytes_accessed=rows_dev * cols_dev * 4,
            transcendentals=0,
        ),
    )

    def new(blocks):
        return pltpu.VMEM((blocks * depth, cols_dev // 2), trailing.dtype)

    solved, early_rows, cols_near, updated = pl.pallas_call(
        functools.partial(update_kernel, n_col, True),
        out_shape=[own, early_rows, cols_near, slab],
        in_specs=[VMEM] * (3 + early),
        out_specs=[HBM, VMEM, VMEM, HBM],
        scratch_shapes=[
            new(early),
            pltpu.SemaphoreType.DMA((early,)),
            pltpu.SemaphoreType.DMA,
        ],
        name="update_first",
        **params,
    )(inverse, near, held, *pieces[:early])
    updated = pl.pallas_call(
        functools.partial(update_kernel, n_col, False),
        out_shape=slab,
        in_specs=[VMEM] * (5 + late) + [HBM],
        out_specs=HBM,
        scratch_shapes=[
            new(n_col + late),
            pltpu.SemaphoreType.DMA((n_col + late,)),
            pltpu.VMEM((cols_dev // 2, width), panel.dtype),
            pltpu.VMEM((late * depth, width), panel.dtype),
        ],
        input_output_aliases={5 + late: 0},
        name="update_second",
        **params,
    )(inverse, other, held, *pieces[early:], early_rows, cols_near, updated)
    return solved, updated


def solution(mesh):
    n_row, n_col = mesh.shape["row"], mesh.shape["col"]
    in_specs = (P("row", None), P(("row", "col"), None), P("row", "col"))
    out_specs = (P(("row", "col"), None), P("row", "col"))

    def step(*args):
        return per_device(n_row, n_col, *args)

    return jax.shard_map(
        step, mesh=mesh, in_specs=in_specs, out_specs=out_specs, check_vma=False
    )
```

```python
import functools

import jax
import jax.numpy as jnp
from jax import lax
from jax.experimental import pallas as pl
from jax.experimental.pallas import tpu as pltpu
from jax.sharding import PartitionSpec as P


SUB = 8
AHEAD = 3

VMEM = pl.BlockSpec(memory_space=pltpu.VMEM)
HBM = pl.BlockSpec(memory_space=pltpu.HBM)


def exchange(value, axis, size, step):
    return lax.ppermute(value, axis, [(i, i ^ step) for i in range(size)])


def far_steps(n_row):
    half = n_row // 2
    return [half] + [i for i in range(n_row - 2, 0, -2) if i != half]


def terms(x):
    out = []
    for _ in range(3):
        out.append(x.astype(jnp.bfloat16).astype(jnp.float32))
        x = x - out[-1]
    return out


def outer_product(x, y):
    x, y = terms(x), terms(y)
    chosen = [(0, 0), (0, 1), (1, 0), (1, 1), (0, 2), (2, 0)]
    left = [x[i] for i, _ in chosen]
    right = [y[j] for _, j in chosen]
    left = jnp.concatenate(left, 0).astype(jnp.bfloat16)
    right = jnp.concatenate(right, 0).astype(jnp.bfloat16)
    return lax.dot_general(
        left, right, (((0,), (0,)), ((), ())), preferred_element_type=jnp.float32
    )


def tree_steps(n_row):
    steps = [n_row // 4]
    while steps[-1] > 2:
        steps.append(steps[-1] // 2)
    return steps


def inverse_factor(tile):
    n = tile[0].shape[1]
    blocks = n // SUB
    rows = list(tile)
    lane = lax.broadcasted_iota(jnp.int32, (SUB, n), 1)
    sub = lax.broadcasted_iota(jnp.int32, (SUB, n), 0)

    def col(x, c):
        return jnp.take_along_axis(x, jnp.full((SUB, n), c, jnp.int32), axis=1)

    def row(x, r):
        return jnp.broadcast_to(x[r : r + 1, :], (SUB, n))

    out = []
    for block in range(blocks):
        base = block * SUB
        inside = (lane >= base) & (lane < base + SUB)
        here = rows[block]
        cols = [col(here, base + j) for j in range(SUB)]
        here = jnp.where(inside, (lane - base == sub).astype(jnp.float32), here)
        near = range(block + 1, min(block + 1 + AHEAD, blocks))
        cols_near = {i: [col(rows[i], base + j) for j in range(SUB)] for i in near}
        for i in near:
            rows[i] = jnp.where(inside, 0.0, rows[i])
        pivots = jnp.zeros((SUB, n), jnp.float32)
        scales = jnp.zeros((SUB, n), jnp.float32)
        for k in range(0, SUB, 2):
            a, b, c = row(cols[k], k), row(cols[k + 1], k), row(cols[k + 1], k + 1)
            det = a * c - b * b
            inv_a = pl.reciprocal(a)
            inv_det = pl.reciprocal(det)
            ratio = b * inv_a
            first = row(here, k)
            second = row(here, k + 1) - ratio * first
            m1 = jnp.where(sub > k, cols[k], 0.0) * inv_a
            m2 = jnp.where(sub > k + 1, a * cols[k + 1] - b * cols[k], 0.0) * inv_det
            n1 = {i: cols_near[i][k] * inv_a for i in near}
            n2 = {i: (a * cols_near[i][k + 1] - b * cols_near[i][k]) * inv_det for i in near}
            pairs = [(row(cols[j], k), row(cols[j], k + 1)) for j in range(k + 2, SUB)]
            for j, (x1, x2) in zip(range(k + 2, SUB), pairs):
                x2 = x2 - ratio * x1
                cols[j] = cols[j] - m1 * x1 - m2 * x2
                for i in near:
                    cols_near[i][j] = cols_near[i][j] - n1[i] * x1 - n2[i] * x2
            here = here - m1 * first - m2 * second
            for i in near:
                rows[i] = rows[i] - n1[i] * first - n2[i] * second
            pivots = jnp.where(sub == k, a, jnp.where(sub == k + 1, det * inv_a, pivots))
            scales = jnp.where(sub == k, inv_a, jnp.where(sub == k + 1, a * inv_det, scales))
        far = range(block + 1 + AHEAD, blocks)
        if far:
            rest = outer_product(here * scales, here)
            for i in far:
                rows[i] = jnp.where(inside, 0.0, rows[i]) - rest[i * SUB : (i + 1) * SUB]
        out.append(jnp.where(lane <= sub + base, here * lax.rsqrt(pivots), 0.0))
    return out


def load_kernel(*refs):
    n = len(refs) // 2
    sems = refs[-1]
    copies = [
        pltpu.make_async_copy(refs[i], refs[n + i], sems.at[i]) for i in range(n)
    ]
    for copy in copies:
        copy.start()
    for copy in copies:
        copy.wait()


def pack_kernel(half, *refs):
    if half:
        tile, tile_beside, panel, panel_beside, two, pack = refs
        odd = lax.rem(lax.axis_index("row"), 2) == 1
        pack[:half, :] = jnp.where(odd, panel_beside[half:, :], panel[:half, :])
    else:
        tile, tile_beside, two = refs
    depth = tile.shape[0]
    for i, ref in enumerate((tile, tile_beside)):
        two[i * depth : (i + 1) * depth, :] = ref[...]
        if half:
            for term, value in enumerate(terms(ref[...])):
                start = half + (2 * term + i) * depth
                pack[start : start + depth, :] = value.astype(jnp.bfloat16)


def inverse_kernel(n_row, half, *refs):
    trailing, *packs, out, held, tile, sem = refs
    load = pltpu.make_async_copy(trailing, held, sem)
    load.start()
    me = lax.axis_index("row")
    depth = tile.shape[0] // n_row
    for step, pack in zip(range(0, n_row, 2), packs):
        for i in range(2):
            if pack.dtype == tile.dtype:
                value = pack[i * depth : (i + 1) * depth, :]
            else:
                parts = []
                for term in range(3):
                    start = half + (2 * term + i) * depth
                    parts.append(pack[start : start + depth, :].astype(jnp.float32))
                value = (parts[0] + parts[1]) + parts[2]
            place = pl.multiple_of((me ^ step ^ i) * depth, depth)
            tile[pl.ds(place, depth), :] = value

    @pl.when(me >= 0)
    def _():
        n = tile.shape[0]
        blocks = inverse_factor([tile[i * SUB : (i + 1) * SUB, :] for i in range(n // SUB)])
        for i in range(0, n // SUB, 2):
            pair = jnp.concatenate([blocks[i], blocks[i + 1]], 0)
            out[i * SUB : (i + 2) * SUB, :] = pair.astype(out.dtype)

    load.wait()


def product(a, b):
    return lax.dot_general(a, b, (((1,), (1,)), ((), ())), preferred_element_type=jnp.float32)


def update_kernel(n_col, first, *refs):
    early = n_col // 2
    count = early if first else n_col - early
    inverse, col_rows, held = refs[:3]
    pieces, refs = refs[3 : 3 + count], refs[3 + count :]
    if first:
        solved, rows_early, cols_near, left, own_sem = refs
    else:
        rows_early, cols_near, left, updated, new, sems, cols_other, rows_late = refs
    row, col = lax.axis_index("row"), lax.axis_index("col")
    rows_dev, cols_dev = held.shape
    width = cols_dev // 2
    depth = rows_dev // n_col
    odd = lax.rem(row, 2)
    lanes_near = pl.multiple_of(odd * width, width)
    lanes_other = pl.multiple_of((1 - odd) * width, width)
    weights = inverse[...]

    def part(i):
        return pl.ds(pl.multiple_of(i * depth, depth), depth)

    def solve(out):
        for i in range(count):
            out[part(i), :] = product(pieces[i][...], weights).astype(out.dtype)

    def block(step, rows, cols, lanes):
        start = pl.multiple_of((col ^ step) * depth, depth)
        update = jnp.dot(rows[...], cols[...], preferred_element_type=jnp.float32)
        ahead = row * rows_dev + start - (col * cols_dev + lanes)
        row_ids = lax.broadcasted_iota(jnp.int32, (depth, width), 0)
        col_ids = lax.broadcasted_iota(jnp.int32, (depth, width), 1)
        old = held[pl.ds(start, depth), pl.ds(lanes, width)]
        return old - jnp.where(col_ids - row_ids <= ahead, update, 0.0)

    def store(step):
        place = pl.ds(pl.multiple_of((col ^ step) * depth, depth), depth)
        return pltpu.make_async_copy(new.at[part(step)], updated.at[place], sems.at[step])

    if first:
        cols_near[...] = product(weights, col_rows[...]).astype(cols_near.dtype)
        solve(rows_early)
        save = pltpu.make_async_copy(rows_early.at[part(0)], solved, own_sem)
        save.start()

        @pl.loop(0, early)
        def _(i):
            left[part(i), :] = block(i, rows_early.at[part(i)], cols_near, lanes_near)

        save.wait()
    else:
        cols_other[...] = product(weights, col_rows[...]).astype(cols_other.dtype)

        @pl.loop(0, early)
        def _(i):
            new[part(i), pl.ds(lanes_near, width)] = left[part(i), :]
            new[part(i), pl.ds(lanes_other, width)] = block(
                i, rows_early.at[part(i)], cols_other, lanes_other
            )
            store(i).start()

        solve(rows_late)

        @pl.loop(0, count)
        def _(i):
            rows = rows_late.at[part(i)]
            for cols, lanes in ((cols_near, lanes_near), (cols_other, lanes_other)):
                new[part(early + i), pl.ds(lanes, width)] = block(early + i, rows, cols, lanes)
            store(early + i).start()

        @pl.loop(0, n_col)
        def _(i):
            store(i).wait()


def column_rows(panel, n_col, cols_dev):
    rows_dev = panel.shape[0] * n_col
    row, start = lax.axis_index("row"), lax.axis_index("col") * cols_dev
    whole = lax.all_gather(panel, "col", axis=0, tiled=True)
    picked = lax.dynamic_slice_in_dim(whole, start % rows_dev, cols_dev, 0)
    kept = jnp.where(row == start // rows_dev, picked, 0).astype(picked.dtype)
    rows = lax.psum(kept, "row")
    half = cols_dev // 2
    odd = row % 2 == 1
    return jnp.where(odd, rows[half:], rows[:half]), jnp.where(odd, rows[:half], rows[half:])


def per_device(n_row, n_col, diag_tile, panel, trailing):
    rows_dev, cols_dev = trailing.shape
    depth, width = panel.shape
    direct = depth == cols_dev and n_col * cols_dev <= rows_dev
    half = depth // 2 if direct else 0
    pieces = []
    for step in range(1, n_col):
        pieces.append(exchange(panel, "col", n_col, step))
    tile_near, panel_near = pl.pallas_call(
        load_kernel,
        out_shape=[jax.ShapeDtypeStruct(a.shape, a.dtype) for a in (diag_tile, panel)],
        in_specs=[HBM] * 2,
        out_specs=[VMEM] * 2,
        scratch_shapes=[pltpu.SemaphoreType.DMA((2,))],
        cost_estimate=pl.CostEstimate(flops=1, bytes_accessed=4 * depth * width, transcendentals=0),
        compiler_params=pltpu.CompilerParams(vmem_limit_bytes=4 * 1024 * 1024),
        name="load",
    )(
        pltpu.with_memory_space_constraint(diag_tile, pltpu.HBM),
        pltpu.with_memory_space_constraint(panel, pltpu.HBM),
    )
    packed = [tile_near, exchange(diag_tile, "row", n_row, 1)]
    outs = [jax.ShapeDtypeStruct((2 * diag_tile.shape[0], width), jnp.float32)]
    if direct:
        packed += [panel_near, exchange(panel, "row", n_row, 1)]
        pack_shape = (half + 6 * diag_tile.shape[0], width)
        outs.append(jax.ShapeDtypeStruct(pack_shape, panel.dtype))
    pieces.insert(0, panel_near)
    two, *pack = pl.pallas_call(
        functools.partial(pack_kernel, half),
        out_shape=outs,
        in_specs=[VMEM] * len(packed),
        out_specs=[VMEM] * len(outs),
        cost_estimate=pl.CostEstimate(flops=1, bytes_accessed=4 * depth * width, transcendentals=0),
        compiler_params=pltpu.CompilerParams(vmem_limit_bytes=4 * 1024 * 1024),
        name="pack",
    )(*packed)
    middle = n_row // 2
    packs = {0: two}
    for step in far_steps(n_row):
        value = pack[0] if direct and step == middle else two
        packs[step] = exchange(value, "row", n_row, step)
    row = lax.axis_index("row")
    if direct:
        near = jnp.where(row & middle != 0, packs[middle][:half], pack[0][:half])
        for step in tree_steps(n_row):
            came = exchange(near, "row", n_row, step)
            near = jnp.where(row & step != 0, came, near)
        other = exchange(near, "row", n_row, 1)
    else:
        near, other = column_rows(panel, n_col, cols_dev)
    packs = [packs[step] for step in range(0, n_row, 2)]
    inverse, held = pl.pallas_call(
        functools.partial(inverse_kernel, n_row, half),
        out_shape=[
            jax.ShapeDtypeStruct((width, width), jnp.bfloat16),
            jax.ShapeDtypeStruct(trailing.shape, trailing.dtype),
        ],
        in_specs=[HBM] + [VMEM] * (n_row // 2),
        out_specs=[VMEM] * 2,
        scratch_shapes=[
            pltpu.VMEM((width, width), jnp.float32),
            pltpu.SemaphoreType.DMA,
        ],
        cost_estimate=pl.CostEstimate(
            flops=2 * width**3, bytes_accessed=width * width * 6, transcendentals=width
        ),
        compiler_params=pltpu.CompilerParams(vmem_limit_bytes=48 * 1024 * 1024),
        name="inverse",
    )(trailing, *packs)

    early = n_col // 2
    late = n_col - early
    slab = jax.ShapeDtypeStruct(trailing.shape, trailing.dtype)
    own = jax.ShapeDtypeStruct(panel.shape, panel.dtype)
    early_rows = jax.ShapeDtypeStruct((early * depth, width), panel.dtype)
    cols_near = jax.ShapeDtypeStruct((width, cols_dev // 2), panel.dtype)
    left = jax.ShapeDtypeStruct((early * depth, cols_dev // 2), trailing.dtype)
    params = dict(
        compiler_params=pltpu.CompilerParams(vmem_limit_bytes=16 * 1024 * 1024),
        cost_estimate=pl.CostEstimate(
            flops=rows_dev * cols_dev * width,
            bytes_accessed=rows_dev * cols_dev * 4,
            transcendentals=0,
        ),
    )
    solved, early_rows, cols_near, left = pl.pallas_call(
        functools.partial(update_kernel, n_col, True),
        out_shape=[own, early_rows, cols_near, left],
        in_specs=[VMEM] * (3 + early),
        out_specs=[HBM, VMEM, VMEM, VMEM],
        scratch_shapes=[pltpu.SemaphoreType.DMA],
        name="update_first",
        **params,
    )(inverse, near, held, *pieces[:early])
    updated = pl.pallas_call(
        functools.partial(update_kernel, n_col, False),
        out_shape=slab,
        in_specs=[VMEM] * (6 + late),
        out_specs=HBM,
        scratch_shapes=[
            pltpu.VMEM(trailing.shape, trailing.dtype),
            pltpu.SemaphoreType.DMA((n_col,)),
            pltpu.VMEM((width, cols_dev // 2), panel.dtype),
            pltpu.VMEM((late * depth, width), panel.dtype),
        ],
        name="update_second",
        **params,
    )(inverse, other, held, *pieces[early:], early_rows, cols_near, left)
    return solved, updated


def solution(mesh):
    n_row, n_col = mesh.shape["row"], mesh.shape["col"]
    in_specs = (P("row", None), P(("row", "col"), None), P("row", "col"))
    out_specs = (P(("row", "col"), None), P("row", "col"))

    def step(*args):
        return per_device(n_row, n_col, *args)

    return jax.shard_map(
        step, mesh=mesh, in_specs=in_specs, out_specs=out_specs, check_vma=False
    )
```

```python
import functools

import jax
import jax.numpy as jnp
from jax import lax
from jax.experimental import pallas as pl
from jax.experimental.pallas import tpu as pltpu
from jax.sharding import PartitionSpec as P


SUB = 8
AHEAD = 3

VMEM = pl.BlockSpec(memory_space=pltpu.VMEM)
HBM = pl.BlockSpec(memory_space=pltpu.HBM)


def exchange(value, axis, size, step):
    return lax.ppermute(value, axis, [(i, i ^ step) for i in range(size)])


def far_steps(n_row):
    half = n_row // 2
    return [half] + [i for i in range(n_row - 2, 0, -2) if i != half]


def terms(x):
    out = []
    for _ in range(3):
        out.append(x.astype(jnp.bfloat16).astype(jnp.float32))
        x = x - out[-1]
    return out


def outer_product(x, y):
    x, y = terms(x), terms(y)
    chosen = [(0, 0), (0, 1), (1, 0), (1, 1), (0, 2), (2, 0)]
    left = [x[i] for i, _ in chosen]
    right = [y[j] for _, j in chosen]
    left = jnp.concatenate(left, 0).astype(jnp.bfloat16)
    right = jnp.concatenate(right, 0).astype(jnp.bfloat16)
    return lax.dot_general(
        left, right, (((0,), (0,)), ((), ())), preferred_element_type=jnp.float32
    )


def tree_steps(n_row):
    steps = [n_row // 4]
    while steps[-1] > 2:
        steps.append(steps[-1] // 2)
    return steps


def inverse_factor(tile):
    n = tile[0].shape[1]
    blocks = n // SUB
    rows = list(tile)
    lane = lax.broadcasted_iota(jnp.int32, (SUB, n), 1)
    sub = lax.broadcasted_iota(jnp.int32, (SUB, n), 0)

    def col(x, c):
        return jnp.take_along_axis(x, jnp.full((SUB, n), c, jnp.int32), axis=1)

    def row(x, r):
        return jnp.broadcast_to(x[r : r + 1, :], (SUB, n))

    out = []
    for block in range(blocks):
        base = block * SUB
        inside = (lane >= base) & (lane < base + SUB)
        here = rows[block]
        cols = [col(here, base + j) for j in range(SUB)]
        here = jnp.where(inside, (lane - base == sub).astype(jnp.float32), here)
        near = range(block + 1, min(block + 1 + AHEAD, blocks))
        cols_near = {i: [col(rows[i], base + j) for j in range(SUB)] for i in near}
        for i in near:
            rows[i] = jnp.where(inside, 0.0, rows[i])
        pivots = jnp.zeros((SUB, n), jnp.float32)
        scales = jnp.zeros((SUB, n), jnp.float32)
        for k in range(0, SUB, 2):
            a, b, c = row(cols[k], k), row(cols[k + 1], k), row(cols[k + 1], k + 1)
            det = a * c - b * b
            inv_a = pl.reciprocal(a)
            inv_det = pl.reciprocal(det)
            ratio = b * inv_a
            first = row(here, k)
            second = row(here, k + 1) - ratio * first
            m1 = jnp.where(sub > k, cols[k], 0.0) * inv_a
            m2 = jnp.where(sub > k + 1, a * cols[k + 1] - b * cols[k], 0.0) * inv_det
            n1 = {i: cols_near[i][k] * inv_a for i in near}
            n2 = {i: (a * cols_near[i][k + 1] - b * cols_near[i][k]) * inv_det for i in near}
            pairs = [(row(cols[j], k), row(cols[j], k + 1)) for j in range(k + 2, SUB)]
            for j, (x1, x2) in zip(range(k + 2, SUB), pairs):
                x2 = x2 - ratio * x1
                cols[j] = cols[j] - m1 * x1 - m2 * x2
                for i in near:
                    cols_near[i][j] = cols_near[i][j] - n1[i] * x1 - n2[i] * x2
            here = here - m1 * first - m2 * second
            for i in near:
                rows[i] = rows[i] - n1[i] * first - n2[i] * second
            pivots = jnp.where(sub == k, a, jnp.where(sub == k + 1, det * inv_a, pivots))
            scales = jnp.where(sub == k, inv_a, jnp.where(sub == k + 1, a * inv_det, scales))
        far = range(block + 1 + AHEAD, blocks)
        if far:
            rest = outer_product(here * scales, here)
            for i in far:
                rows[i] = jnp.where(inside, 0.0, rows[i]) - rest[i * SUB : (i + 1) * SUB]
        out.append(jnp.where(lane <= sub + base, here * lax.rsqrt(pivots), 0.0))
    return out


def load_kernel(*refs):
    n = len(refs) // 2
    sems = refs[-1]
    copies = [
        pltpu.make_async_copy(refs[i], refs[n + i], sems.at[i]) for i in range(n)
    ]
    for copy in copies:
        copy.start()
    for copy in copies:
        copy.wait()


def pack_kernel(half, *refs):
    if half:
        tile, tile_beside, panel, panel_beside, two, pack = refs
        odd = lax.rem(lax.axis_index("row"), 2) == 1
        pack[:half, :] = jnp.where(odd, panel_beside[half:, :], panel[:half, :])
    else:
        tile, tile_beside, two = refs
    depth = tile.shape[0]
    for i, ref in enumerate((tile, tile_beside)):
        two[i * depth : (i + 1) * depth, :] = ref[...]
        if half:
            for term, value in enumerate(terms(ref[...])):
                start = half + (2 * term + i) * depth
                pack[start : start + depth, :] = value.astype(jnp.bfloat16)


def inverse_kernel(n_row, half, *refs):
    trailing, *packs, out, held, tile, sem = refs
    load = pltpu.make_async_copy(trailing, held, sem)
    load.start()
    me = lax.axis_index("row")
    depth = tile.shape[0] // n_row
    for step, pack in zip(range(0, n_row, 2), packs):
        for i in range(2):
            if pack.dtype == tile.dtype:
                value = pack[i * depth : (i + 1) * depth, :]
            else:
                parts = []
                for term in range(3):
                    start = half + (2 * term + i) * depth
                    parts.append(pack[start : start + depth, :].astype(jnp.float32))
                value = (parts[0] + parts[1]) + parts[2]
            place = pl.multiple_of((me ^ step ^ i) * depth, depth)
            tile[pl.ds(place, depth), :] = value

    @pl.when(me >= 0)
    def _():
        n = tile.shape[0]
        blocks = inverse_factor([tile[i * SUB : (i + 1) * SUB, :] for i in range(n // SUB)])
        for i in range(0, n // SUB, 2):
            pair = jnp.concatenate([blocks[i], blocks[i + 1]], 0)
            out[i * SUB : (i + 2) * SUB, :] = pair.astype(out.dtype)

    load.wait()


def product(a, b):
    return lax.dot_general(a, b, (((1,), (1,)), ((), ())), preferred_element_type=jnp.float32)


def update_kernel(n_col, first, *refs):
    early = n_col // 2
    count = early if first else n_col - early
    inverse, col_rows, held = refs[:3]
    pieces, refs = refs[3 : 3 + count], refs[3 + count :]
    if first:
        solved, rows_early, cols_near, left, own_sem = refs
    else:
        rows_early, cols_near, left, updated, new, sems, cols_other, rows_late = refs
    row, col = lax.axis_index("row"), lax.axis_index("col")
    rows_dev, cols_dev = held.shape
    width = cols_dev // 2
    depth = rows_dev // n_col
    odd = lax.rem(row, 2)
    lanes_near = pl.multiple_of(odd * width, width)
    lanes_other = pl.multiple_of((1 - odd) * width, width)
    weights = inverse[...]

    def part(i):
        return pl.ds(pl.multiple_of(i * depth, depth), depth)

    def solve(out):
        for i in range(count):
            out[part(i), :] = product(pieces[i][...], weights).astype(out.dtype)

    def block(step, rows, cols, lanes):
        start = pl.multiple_of((col ^ step) * depth, depth)
        update = jnp.dot(rows[...], cols[...], preferred_element_type=jnp.float32)
        ahead = row * rows_dev + start - (col * cols_dev + lanes)
        row_ids = lax.broadcasted_iota(jnp.int32, (depth, width), 0)
        col_ids = lax.broadcasted_iota(jnp.int32, (depth, width), 1)
        old = held[pl.ds(start, depth), pl.ds(lanes, width)]
        return old - jnp.where(col_ids - row_ids <= ahead, update, 0.0)

    def store(step):
        place = pl.ds(pl.multiple_of((col ^ step) * depth, depth), depth)
        return pltpu.make_async_copy(new.at[part(step)], updated.at[place], sems.at[step])

    if first:
        cols_near[...] = product(weights, col_rows[...]).astype(cols_near.dtype)
        solve(rows_early)
        save = pltpu.make_async_copy(rows_early.at[part(0)], solved, own_sem)
        save.start()

        @pl.loop(0, early)
        def _(i):
            left[part(i), :] = block(i, rows_early.at[part(i)], cols_near, lanes_near)

        save.wait()
    else:
        cols_other[...] = product(weights, col_rows[...]).astype(cols_other.dtype)

        @pl.loop(0, early)
        def _(i):
            new[part(i), pl.ds(lanes_near, width)] = left[part(i), :]
            new[part(i), pl.ds(lanes_other, width)] = block(
                i, rows_early.at[part(i)], cols_other, lanes_other
            )
            store(i).start()

        solve(rows_late)

        @pl.loop(0, count)
        def _(i):
            rows = rows_late.at[part(i)]
            for cols, lanes in ((cols_near, lanes_near), (cols_other, lanes_other)):
                new[part(early + i), pl.ds(lanes, width)] = block(early + i, rows, cols, lanes)
            store(early + i).start()

        @pl.loop(0, n_col)
        def _(i):
            store(i).wait()


def column_rows(panel, n_col, cols_dev):
    rows_dev = panel.shape[0] * n_col
    row, start = lax.axis_index("row"), lax.axis_index("col") * cols_dev
    whole = lax.all_gather(panel, "col", axis=0, tiled=True)
    picked = lax.dynamic_slice_in_dim(whole, start % rows_dev, cols_dev, 0)
    kept = jnp.where(row == start // rows_dev, picked, 0).astype(picked.dtype)
    rows = lax.psum(kept, "row")
    half = cols_dev // 2
    odd = row % 2 == 1
    return jnp.where(odd, rows[half:], rows[:half]), jnp.where(odd, rows[:half], rows[half:])


def per_device(n_row, n_col, diag_tile, panel, trailing):
    rows_dev, cols_dev = trailing.shape
    depth, width = panel.shape
    direct = depth == cols_dev and n_col * cols_dev <= rows_dev
    half = depth // 2 if direct else 0
    tile_near, panel_near = pl.pallas_call(
        load_kernel,
        out_shape=[jax.ShapeDtypeStruct(a.shape, a.dtype) for a in (diag_tile, panel)],
        in_specs=[HBM] * 2,
        out_specs=[VMEM] * 2,
        scratch_shapes=[pltpu.SemaphoreType.DMA((2,))],
        cost_estimate=pl.CostEstimate(flops=1, bytes_accessed=4 * depth * width, transcendentals=0),
        compiler_params=pltpu.CompilerParams(vmem_limit_bytes=4 * 1024 * 1024),
        name="load",
    )(
        pltpu.with_memory_space_constraint(diag_tile, pltpu.HBM),
        pltpu.with_memory_space_constraint(panel, pltpu.HBM),
    )
    packed = [tile_near, exchange(diag_tile, "row", n_row, 1)]
    outs = [jax.ShapeDtypeStruct((2 * diag_tile.shape[0], width), jnp.float32)]
    if direct:
        packed += [panel_near, exchange(panel, "row", n_row, 1)]
        pack_shape = (half + 6 * diag_tile.shape[0], width)
        outs.append(jax.ShapeDtypeStruct(pack_shape, panel.dtype))
    pieces = [panel_near]
    for step in range(1, n_col):
        pieces.append(exchange(panel_near, "col", n_col, step))
    two, *pack = pl.pallas_call(
        functools.partial(pack_kernel, half),
        out_shape=outs,
        in_specs=[VMEM] * len(packed),
        out_specs=[VMEM] * len(outs),
        cost_estimate=pl.CostEstimate(flops=1, bytes_accessed=4 * depth * width, transcendentals=0),
        compiler_params=pltpu.CompilerParams(vmem_limit_bytes=4 * 1024 * 1024),
        name="pack",
    )(*packed)
    middle = n_row // 2
    packs = {0: two}
    for step in far_steps(n_row):
        value = pack[0] if direct and step == middle else two
        packs[step] = exchange(value, "row", n_row, step)
    row = lax.axis_index("row")
    if direct:
        near = jnp.where(row & middle != 0, packs[middle][:half], pack[0][:half])
        for step in tree_steps(n_row):
            came = exchange(near, "row", n_row, step)
            near = jnp.where(row & step != 0, came, near)
        other = exchange(near, "row", n_row, 1)
    else:
        near, other = column_rows(panel, n_col, cols_dev)
    packs = [packs[step] for step in range(0, n_row, 2)]
    inverse, held = pl.pallas_call(
        functools.partial(inverse_kernel, n_row, half),
        out_shape=[
            jax.ShapeDtypeStruct((width, width), jnp.bfloat16),
            jax.ShapeDtypeStruct(trailing.shape, trailing.dtype),
        ],
        in_specs=[HBM] + [VMEM] * (n_row // 2),
        out_specs=[VMEM] * 2,
        scratch_shapes=[
            pltpu.VMEM((width, width), jnp.float32),
            pltpu.SemaphoreType.DMA,
        ],
        cost_estimate=pl.CostEstimate(
            flops=2 * width**3, bytes_accessed=width * width * 6, transcendentals=width
        ),
        compiler_params=pltpu.CompilerParams(vmem_limit_bytes=48 * 1024 * 1024),
        name="inverse",
    )(trailing, *packs)

    early = n_col // 2
    late = n_col - early
    slab = jax.ShapeDtypeStruct(trailing.shape, trailing.dtype)
    own = jax.ShapeDtypeStruct(panel.shape, panel.dtype)
    early_rows = jax.ShapeDtypeStruct((early * depth, width), panel.dtype)
    cols_near = jax.ShapeDtypeStruct((width, cols_dev // 2), panel.dtype)
    left = jax.ShapeDtypeStruct((early * depth, cols_dev // 2), trailing.dtype)
    params = dict(
        compiler_params=pltpu.CompilerParams(vmem_limit_bytes=16 * 1024 * 1024),
        cost_estimate=pl.CostEstimate(
            flops=rows_dev * cols_dev * width,
            bytes_accessed=rows_dev * cols_dev * 4,
            transcendentals=0,
        ),
    )
    solved, early_rows, cols_near, left = pl.pallas_call(
        functools.partial(update_kernel, n_col, True),
        out_shape=[own, early_rows, cols_near, left],
        in_specs=[VMEM] * (3 + early),
        out_specs=[HBM, VMEM, VMEM, VMEM],
        scratch_shapes=[pltpu.SemaphoreType.DMA],
        name="update_first",
        **params,
    )(inverse, near, held, *pieces[:early])
    updated = pl.pallas_call(
        functools.partial(update_kernel, n_col, False),
        out_shape=slab,
        in_specs=[VMEM] * (6 + late),
        out_specs=HBM,
        scratch_shapes=[
            pltpu.VMEM(trailing.shape, trailing.dtype),
            pltpu.SemaphoreType.DMA((n_col,)),
            pltpu.VMEM((width, cols_dev // 2), panel.dtype),
            pltpu.VMEM((late * depth, width), panel.dtype),
        ],
        name="update_second",
        **params,
    )(inverse, other, held, *pieces[early:], early_rows, cols_near, left)
    return solved, updated


def solution(mesh):
    n_row, n_col = mesh.shape["row"], mesh.shape["col"]
    in_specs = (P("row", None), P(("row", "col"), None), P("row", "col"))
    out_specs = (P(("row", "col"), None), P("row", "col"))

    def step(*args):
        return per_device(n_row, n_col, *args)

    return jax.shard_map(
        step, mesh=mesh, in_specs=in_specs, out_specs=out_specs, check_vma=False
    )
```

```python
import functools

import jax
import jax.numpy as jnp
from jax import lax
from jax.experimental import pallas as pl
from jax.experimental.pallas import tpu as pltpu
from jax.sharding import PartitionSpec as P


SUB = 8
AHEAD = 3

VMEM = pl.BlockSpec(memory_space=pltpu.VMEM)
HBM = pl.BlockSpec(memory_space=pltpu.HBM)


def exchange(value, axis, size, step):
    return lax.ppermute(value, axis, [(i, i ^ step) for i in range(size)])


def far_steps(n_row):
    half = n_row // 2
    return [half] + [i for i in range(n_row - 2, 0, -2) if i != half]


def terms(x):
    out = []
    for _ in range(3):
        out.append(x.astype(jnp.bfloat16).astype(jnp.float32))
        x = x - out[-1]
    return out


def outer_product(x, y):
    x, y = terms(x), terms(y)
    chosen = [(0, 0), (0, 1), (1, 0), (1, 1), (0, 2), (2, 0)]
    left = [x[i] for i, _ in chosen]
    right = [y[j] for _, j in chosen]
    left = jnp.concatenate(left, 0).astype(jnp.bfloat16)
    right = jnp.concatenate(right, 0).astype(jnp.bfloat16)
    return lax.dot_general(
        left, right, (((0,), (0,)), ((), ())), preferred_element_type=jnp.float32
    )


def paired_steps(n_row):
    return len(far_steps(n_row)) == 3


def exchange_far(value, n_row):
    pairs = [(i, i ^ (n_row - 2 if i % 2 else n_row // 2)) for i in range(n_row)]
    return lax.ppermute(value, "row", pairs)


def inverse_factor(tile):
    n = tile[0].shape[1]
    blocks = n // SUB
    rows = list(tile)
    lane = lax.broadcasted_iota(jnp.int32, (SUB, n), 1)
    sub = lax.broadcasted_iota(jnp.int32, (SUB, n), 0)

    def col(x, c):
        return jnp.take_along_axis(x, jnp.full((SUB, n), c, jnp.int32), axis=1)

    def row(x, r):
        return jnp.broadcast_to(x[r : r + 1, :], (SUB, n))

    out = []
    for block in range(blocks):
        base = block * SUB
        inside = (lane >= base) & (lane < base + SUB)
        here = rows[block]
        cols = [col(here, base + j) for j in range(SUB)]
        here = jnp.where(inside, (lane - base == sub).astype(jnp.float32), here)
        near = range(block + 1, min(block + 1 + AHEAD, blocks))
        cols_near = {i: [col(rows[i], base + j) for j in range(SUB)] for i in near}
        for i in near:
            rows[i] = jnp.where(inside, 0.0, rows[i])
        pivots = jnp.zeros((SUB, n), jnp.float32)
        scales = jnp.zeros((SUB, n), jnp.float32)
        for k in range(0, SUB, 2):
            a, b, c = row(cols[k], k), row(cols[k + 1], k), row(cols[k + 1], k + 1)
            det = a * c - b * b
            inv_a = pl.reciprocal(a)
            inv_det = pl.reciprocal(det)
            ratio = b * inv_a
            first = row(here, k)
            second = row(here, k + 1) - ratio * first
            m1 = jnp.where(sub > k, cols[k], 0.0) * inv_a
            m2 = jnp.where(sub > k + 1, a * cols[k + 1] - b * cols[k], 0.0) * inv_det
            n1 = {i: cols_near[i][k] * inv_a for i in near}
            n2 = {i: (a * cols_near[i][k + 1] - b * cols_near[i][k]) * inv_det for i in near}
            pairs = [(row(cols[j], k), row(cols[j], k + 1)) for j in range(k + 2, SUB)]
            for j, (x1, x2) in zip(range(k + 2, SUB), pairs):
                x2 = x2 - ratio * x1
                cols[j] = cols[j] - m1 * x1 - m2 * x2
                for i in near:
                    cols_near[i][j] = cols_near[i][j] - n1[i] * x1 - n2[i] * x2
            here = here - m1 * first - m2 * second
            for i in near:
                rows[i] = rows[i] - n1[i] * first - n2[i] * second
            pivots = jnp.where(sub == k, a, jnp.where(sub == k + 1, det * inv_a, pivots))
            scales = jnp.where(sub == k, inv_a, jnp.where(sub == k + 1, a * inv_det, scales))
        far = range(block + 1 + AHEAD, blocks)
        if far:
            rest = outer_product(here * scales, here)
            for i in far:
                rows[i] = jnp.where(inside, 0.0, rows[i]) - rest[i * SUB : (i + 1) * SUB]
        out.append(jnp.where(lane <= sub + base, here * lax.rsqrt(pivots), 0.0))
    return out


def load_kernel(*refs):
    n = len(refs) // 2
    sems = refs[-1]
    copies = [
        pltpu.make_async_copy(refs[i], refs[n + i], sems.at[i]) for i in range(n)
    ]
    for copy in copies:
        copy.start()
    for copy in copies:
        copy.wait()


def pack_kernel(half, *refs):
    if half:
        tile, tile_beside, panel, panel_beside, two, pack = refs
        odd = lax.rem(lax.axis_index("row"), 2) == 1
        pack[:half, :] = jnp.where(odd, panel_beside[half:, :], panel[:half, :])
    else:
        tile, tile_beside, two = refs
    depth = tile.shape[0]
    for i, ref in enumerate((tile, tile_beside)):
        two[i * depth : (i + 1) * depth, :] = ref[...]
        if half:
            for term, value in enumerate(terms(ref[...])):
                start = half + (2 * term + i) * depth
                pack[start : start + depth, :] = value.astype(jnp.bfloat16)


def inverse_kernel(steps, *refs):
    trailing, *packs, out, held, tile, sem = refs
    load = pltpu.make_async_copy(trailing, held, sem)
    load.start()
    me = lax.axis_index("row")
    odd = lax.rem(me, 2)
    depth = packs[0].shape[0] // 2
    for (step, turn, crossed), pack in zip(steps, packs):
        step = step + odd * turn
        for i in range(2):
            if pack.dtype == tile.dtype:
                value = pack[i * depth : (i + 1) * depth, :]
            else:
                parts = []
                for term in range(3):
                    start = pack.shape[0] - (6 - 2 * term - i) * depth
                    parts.append(pack[start : start + depth, :].astype(jnp.float32))
                value = (parts[0] + parts[1]) + parts[2]
            place = pl.multiple_of((me ^ step ^ (i ^ crossed)) * depth, depth)
            tile[pl.ds(place, depth), :] = value

    @pl.when(me >= 0)
    def _():
        n = tile.shape[0]
        blocks = inverse_factor([tile[i * SUB : (i + 1) * SUB, :] for i in range(n // SUB)])
        for i in range(0, n // SUB, 2):
            pair = jnp.concatenate([blocks[i], blocks[i + 1]], 0)
            out[i * SUB : (i + 2) * SUB, :] = pair.astype(out.dtype)

    load.wait()


def product(a, b):
    return lax.dot_general(a, b, (((1,), (1,)), ((), ())), preferred_element_type=jnp.float32)


def update_kernel(n_col, first, *refs):
    early = n_col // 2
    count = early if first else n_col - early
    inverse, col_rows, held = refs[:3]
    pieces, refs = refs[3 : 3 + count], refs[3 + count :]
    if first:
        solved, rows_early, cols_near, left, own_sem = refs
    else:
        rows_early, cols_near, left, updated, new, sems, cols_other, rows_late = refs
    row, col = lax.axis_index("row"), lax.axis_index("col")
    rows_dev, cols_dev = held.shape
    width = cols_dev // 2
    depth = rows_dev // n_col
    odd = lax.rem(row, 2)
    lanes_near = pl.multiple_of(odd * width, width)
    lanes_other = pl.multiple_of((1 - odd) * width, width)
    weights = inverse[...]

    def part(i):
        return pl.ds(pl.multiple_of(i * depth, depth), depth)

    def solve(out):
        for i in range(count):
            out[part(i), :] = product(pieces[i][...], weights).astype(out.dtype)

    def block(step, rows, cols, lanes):
        start = pl.multiple_of((col ^ step) * depth, depth)
        update = jnp.dot(rows[...], cols[...], preferred_element_type=jnp.float32)
        ahead = row * rows_dev + start - (col * cols_dev + lanes)
        row_ids = lax.broadcasted_iota(jnp.int32, (depth, width), 0)
        col_ids = lax.broadcasted_iota(jnp.int32, (depth, width), 1)
        old = held[pl.ds(start, depth), pl.ds(lanes, width)]
        return old - jnp.where(col_ids - row_ids <= ahead, update, 0.0)

    def store(step):
        place = pl.ds(pl.multiple_of((col ^ step) * depth, depth), depth)
        return pltpu.make_async_copy(new.at[part(step)], updated.at[place], sems.at[step])

    if first:
        cols_near[...] = product(weights, col_rows[...]).astype(cols_near.dtype)
        solve(rows_early)
        save = pltpu.make_async_copy(rows_early.at[part(0)], solved, own_sem)
        save.start()

        @pl.loop(0, early)
        def _(i):
            left[part(i), :] = block(i, rows_early.at[part(i)], cols_near, lanes_near)

        save.wait()
    else:
        cols_other[...] = product(weights, col_rows[...]).astype(cols_other.dtype)

        @pl.loop(0, early)
        def _(i):
            new[part(i), pl.ds(lanes_near, width)] = left[part(i), :]
            new[part(i), pl.ds(lanes_other, width)] = block(
                i, rows_early.at[part(i)], cols_other, lanes_other
            )
            store(i).start()

        solve(rows_late)

        @pl.loop(0, count)
        def _(i):
            rows = rows_late.at[part(i)]
            for cols, lanes in ((cols_near, lanes_near), (cols_other, lanes_other)):
                new[part(early + i), pl.ds(lanes, width)] = block(early + i, rows, cols, lanes)
            store(early + i).start()

        @pl.loop(0, n_col)
        def _(i):
            store(i).wait()


def column_rows(panel, n_col, cols_dev):
    rows_dev = panel.shape[0] * n_col
    row, start = lax.axis_index("row"), lax.axis_index("col") * cols_dev
    whole = lax.all_gather(panel, "col", axis=0, tiled=True)
    picked = lax.dynamic_slice_in_dim(whole, start % rows_dev, cols_dev, 0)
    kept = jnp.where(row == start // rows_dev, picked, 0).astype(picked.dtype)
    rows = lax.psum(kept, "row")
    half = cols_dev // 2
    odd = row % 2 == 1
    return jnp.where(odd, rows[half:], rows[:half]), jnp.where(odd, rows[:half], rows[half:])


def per_device(n_row, n_col, diag_tile, panel, trailing):
    rows_dev, cols_dev = trailing.shape
    depth, width = panel.shape
    direct = depth == cols_dev and n_col * cols_dev <= rows_dev and paired_steps(n_row)
    half = depth // 2 if direct else 0
    tile_near, panel_near = pl.pallas_call(
        load_kernel,
        out_shape=[jax.ShapeDtypeStruct(a.shape, a.dtype) for a in (diag_tile, panel)],
        in_specs=[HBM] * 2,
        out_specs=[VMEM] * 2,
        scratch_shapes=[pltpu.SemaphoreType.DMA((2,))],
        cost_estimate=pl.CostEstimate(flops=1, bytes_accessed=4 * depth * width, transcendentals=0),
        compiler_params=pltpu.CompilerParams(vmem_limit_bytes=4 * 1024 * 1024),
        name="load",
    )(
        pltpu.with_memory_space_constraint(diag_tile, pltpu.HBM),
        pltpu.with_memory_space_constraint(panel, pltpu.HBM),
    )
    packed = [tile_near, exchange(diag_tile, "row", n_row, 1)]
    outs = [jax.ShapeDtypeStruct((2 * diag_tile.shape[0], width), jnp.float32)]
    if direct:
        packed += [panel_near, exchange(panel, "row", n_row, 1)]
        pack_shape = (half + 6 * diag_tile.shape[0], width)
        outs.append(jax.ShapeDtypeStruct(pack_shape, panel.dtype))
    pieces = [panel_near]
    for step in range(1, n_col):
        pieces.append(exchange(panel_near, "col", n_col, step))
    two, *pack = pl.pallas_call(
        functools.partial(pack_kernel, half),
        out_shape=outs,
        in_specs=[VMEM] * len(packed),
        out_specs=[VMEM] * len(outs),
        cost_estimate=pl.CostEstimate(flops=1, bytes_accessed=4 * depth * width, transcendentals=0),
        compiler_params=pltpu.CompilerParams(vmem_limit_bytes=4 * 1024 * 1024),
        name="pack",
    )(*packed)
    row = lax.axis_index("row")
    odd = row % 2 == 1
    packs, steps = [two], [(0, 0, 0)]
    if direct:
        middle, last = n_row // 2, n_row - 2
        came = exchange_far(pack[0], n_row)
        packs.append(exchange(two, "row", n_row, 2))
        packs += [came, exchange(came[half:], "row", n_row, 1)]
        steps += [(2, 0, 0), (middle, last - middle, 0), (last, middle - last, 1)]
        chip = row & ~1
        reached = jnp.where(odd, last, middle)
        near = jnp.where(chip == reached, came[:half], pack[0][:half])
        came = exchange(near, "row", n_row, 2)
        near = jnp.where((chip == 2) | (chip == (reached ^ 2)), came, near)
        other = exchange(near, "row", n_row, 1)
    else:
        for step in far_steps(n_row):
            packs.append(exchange(two, "row", n_row, step))
            steps.append((step, 0, 0))
        near, other = column_rows(panel, n_col, cols_dev)
    inverse, held = pl.pallas_call(
        functools.partial(inverse_kernel, steps),
        out_shape=[
            jax.ShapeDtypeStruct((width, width), jnp.bfloat16),
            jax.ShapeDtypeStruct(trailing.shape, trailing.dtype),
        ],
        in_specs=[HBM] + [VMEM] * len(packs),
        out_specs=[VMEM] * 2,
        scratch_shapes=[
            pltpu.VMEM((width, width), jnp.float32),
            pltpu.SemaphoreType.DMA,
        ],
        cost_estimate=pl.CostEstimate(
            flops=2 * width**3, bytes_accessed=width * width * 6, transcendentals=width
        ),
        compiler_params=pltpu.CompilerParams(vmem_limit_bytes=48 * 1024 * 1024),
        name="inverse",
    )(trailing, *packs)

    early = n_col // 2
    late = n_col - early
    slab = jax.ShapeDtypeStruct(trailing.shape, trailing.dtype)
    own = jax.ShapeDtypeStruct(panel.shape, panel.dtype)
    early_rows = jax.ShapeDtypeStruct((early * depth, width), panel.dtype)
    cols_near = jax.ShapeDtypeStruct((width, cols_dev // 2), panel.dtype)
    left = jax.ShapeDtypeStruct((early * depth, cols_dev // 2), trailing.dtype)
    params = dict(
        compiler_params=pltpu.CompilerParams(vmem_limit_bytes=16 * 1024 * 1024),
        cost_estimate=pl.CostEstimate(
            flops=rows_dev * cols_dev * width,
            bytes_accessed=rows_dev * cols_dev * 4,
            transcendentals=0,
        ),
    )
    solved, early_rows, cols_near, left = pl.pallas_call(
        functools.partial(update_kernel, n_col, True),
        out_shape=[own, early_rows, cols_near, left],
        in_specs=[VMEM] * (3 + early),
        out_specs=[HBM, VMEM, VMEM, VMEM],
        scratch_shapes=[pltpu.SemaphoreType.DMA],
        name="update_first",
        **params,
    )(inverse, near, held, *pieces[:early])
    updated = pl.pallas_call(
        functools.partial(update_kernel, n_col, False),
        out_shape=slab,
        in_specs=[VMEM] * (6 + late),
        out_specs=HBM,
        scratch_shapes=[
            pltpu.VMEM(trailing.shape, trailing.dtype),
            pltpu.SemaphoreType.DMA((n_col,)),
            pltpu.VMEM((width, cols_dev // 2), panel.dtype),
            pltpu.VMEM((late * depth, width), panel.dtype),
        ],
        name="update_second",
        **params,
    )(inverse, other, held, *pieces[early:], early_rows, cols_near, left)
    return solved, updated


def solution(mesh):
    n_row, n_col = mesh.shape["row"], mesh.shape["col"]
    in_specs = (P("row", None), P(("row", "col"), None), P("row", "col"))
    out_specs = (P(("row", "col"), None), P("row", "col"))

    def step(*args):
        return per_device(n_row, n_col, *args)

    return jax.shard_map(
        step, mesh=mesh, in_specs=in_specs, out_specs=out_specs, check_vma=False
    )
```
